512 devices in a mesh: depth: 16 (over z, core), rows: 32 (over y, x).
Axes of the slice: x: 4, y: 8, z: 8, core: 2. Of those that a mesh axis runs over, the one named last changes fastest.
Arguments:
- in_flight: float32 [16, 2, 1024, 1024], P('depth', None, 'rows'), may hold values from -6 to 6
- phase_index: bfloat16 [32, 1024, 1024], P('depth', 'rows'), may hold values from -2 to 2
- absorption: bfloat16 [32, 1024, 1024], P('depth', 'rows'), may hold values from 0.099609375 to 2
Outputs:
- exits: float32 [16, 2, 1024, 1024], P('depth', None, 'rows')
The draws below stay inside these ranges and needn't reach their ends.
All inputs are finite; a program needn't handle non-finite values.
Results may differ from the reference program's by a relative error of at most 0.0003.
Values may be sent and summed in bfloat16 or wider, within the bound.
A program may use at most 64 MiB of HBM per device.

```python
import math
import jax
import jax.numpy as jnp
from jax import lax

NXY = 1024
SLICES = 2
TAYLOR = 4
TICKS = 2
GROUPS = 16
LAYERS = 32


def level_of(rng, extent, pieces, smallest, largest):
    def one(axis_at, shards_of):
        heights = jax.random.uniform(jax.random.fold_in(jax.random.fold_in(rng, 6), axis_at), (shards_of,), jnp.float32, smallest / len(pieces), largest / len(pieces))
        return jnp.repeat(jnp.exp(heights), extent[axis_at] // shards_of).reshape((-1,) + (1,) * (len(extent) - axis_at - 1))

    loudness = one(*pieces[0])
    for cut in pieces[1:]:
        loudness = loudness * one(*cut)
    return loudness


def bell_draw(rng, extent, deviation, reach, split=(), kind=jnp.bfloat16):
    gain = level_of(rng, extent, split, -0.22, 0.18) if split else 1.0
    array = jax.random.normal(rng, extent, jnp.float32) * deviation * gain
    return jnp.minimum(jnp.maximum(array, -reach), reach).astype(kind)


def setup_inputs(seed: int = 0) -> dict:
    key_of = jax.random.split(jax.random.key(seed), 4)
    in_flight = bell_draw(key_of[0], (GROUPS, 2, NXY, NXY), 1.0, 6.0, ((0, 16), (2, 32)), jnp.float32)
    phase_index = bell_draw(key_of[1], (LAYERS, NXY, NXY), 0.5, 2.0, ((0, 16), (1, 32)))
    absorption = jnp.clip(jnp.exp(math.log(2.0) - 2.9996462 * jax.random.uniform(key_of[2], (LAYERS, NXY, NXY), jnp.float32) ** level_of(key_of[2], (LAYERS, NXY, NXY), ((0, 16), (1, 32)), -0.2, 0.2)), 0.099609375, 2.0).astype(jnp.bfloat16)
    return {"in_flight": in_flight, "phase_index": phase_index, "absorption": absorption}


lateral = 0.22
contrast = 0.2


def laplace(values):
    padded = jnp.pad(values, ((0, 0), (1, 1), (1, 1)))
    return padded[:, 2:, 1:-1] + padded[:, :-2, 1:-1] + padded[:, 1:-1, 2:] + padded[:, 1:-1, :-2] - 4.0 * values


def generator(values, index_part, loss_part):
    stirred = lateral * laplace(values) + contrast * index_part * values
    damping = contrast * loss_part
    return jnp.stack([-stirred[1] - damping * values[0], stirred[0] - damping * values[1]])


def slice_step(values, index_part, loss_part):
    summed = values
    term_now = values
    for degree in range(1, TAYLOR + 1):
        term_now = generator(term_now, index_part, loss_part) / degree
        summed = summed + term_now
    return summed


def fresnel(length):
    frequency = jnp.arange(length, dtype=jnp.int32)
    frequency = jnp.where(frequency < length // 2, frequency, frequency - length)
    phase_angle = ((frequency * frequency) % (8 * length)).astype(jnp.float32) * (math.pi / (4 * length))
    return lax.complex(jnp.cos(phase_angle), -jnp.sin(phase_angle))


def gap(values):
    spectrum = jnp.fft.fft2(lax.complex(values[0], values[1]))
    kernel = fresnel(NXY)
    spectrum = spectrum * kernel[:, None] * kernel[None, :]
    result = jnp.fft.ifft2(spectrum)
    return jnp.stack([jnp.real(result), jnp.imag(result)])


def group_pass(inputs):
    values, deltas, absorbs = inputs
    for slice_index in range(SLICES):
        values = slice_step(values, deltas[slice_index].astype(jnp.float32), absorbs[slice_index].astype(jnp.float32))
    return gap(values)


def reference(in_flight, phase_index, absorption):
    deltas = phase_index.reshape(GROUPS, SLICES, NXY, NXY)
    absorbs = absorption.reshape(GROUPS, SLICES, NXY, NXY)
    fields = in_flight
    for tick_index in range(TICKS):
        if tick_index > 0:
            fields = jnp.roll(fields, 1, axis=0)
        fields = lax.map(group_pass, (fields, deltas, absorbs))
    return fields
```

```python
import functools
import math

import jax
import jax.numpy as jnp
import ml_dtypes
import numpy as np
from jax import lax
from jax.experimental import pallas as pl
from jax.experimental.pallas import tpu as pltpu
from jax.sharding import PartitionSpec as P

TAYLOR = 4
SLICES = 2
HALO = 8
LANES = 128
lateral = 0.22
contrast = 0.2
MESH = pl.DeviceIdType.MESH


def middle_matrices(length):
    coarse = length // LANES
    b = np.arange(LANES)
    k = np.arange(length)
    f = np.where(k < length // 2, k, k - length)
    gain = np.exp(-1j * np.pi * ((f * f) % (8 * length)) / (4 * length))
    dft = np.exp(-2j * np.pi * (np.outer(b, b) % LANES) / LANES)
    whole = np.zeros((coarse, 2 * LANES, 2 * LANES))
    for k1 in range(coarse):
        twiddle = np.exp(-2j * np.pi * b * k1 / length)
        m = (twiddle[:, None] * dft * gain[k1 + coarse * b][None, :]) @ (np.conj(dft) * np.conj(twiddle)[None, :])
        m = m / length
        whole[k1] = np.block([[m.real, m.imag], [-m.imag, m.real]])
    high = whole.astype(np.float32).astype(ml_dtypes.bfloat16)
    low = (whole - high.astype(np.float64)).astype(np.float32).astype(ml_dtypes.bfloat16)
    return high, low


def radix8(re, im, sign):
    half = math.sqrt(0.5)

    def turn(r, i):
        return (-i, r) if sign > 0 else (i, -r)

    def four(r, i):
        a, b = (r[0] + r[2], i[0] + i[2]), (r[0] - r[2], i[0] - i[2])
        c, d = (r[1] + r[3], i[1] + i[3]), (r[1] - r[3], i[1] - i[3])
        d = turn(*d)
        return [(a[0] + c[0], a[1] + c[1]), (b[0] + d[0], b[1] + d[1]), (a[0] - c[0], a[1] - c[1]), (b[0] - d[0], b[1] - d[1])]

    even = four(re[0::2], im[0::2])
    odd = four(re[1::2], im[1::2])
    s = 1.0 if sign > 0 else -1.0
    o1, o3 = odd[1], odd[3]
    odd[1] = ((o1[0] - s * o1[1]) * half, (o1[1] + s * o1[0]) * half)
    odd[2] = turn(*odd[2])
    odd[3] = ((-o3[0] - s * o3[1]) * half, (-o3[1] + s * o3[0]) * half)
    out = [(e[0] + o[0], e[1] + o[1]) for e, o in zip(even, odd)]
    out += [(e[0] - o[0], e[1] - o[1]) for e, o in zip(even, odd)]
    return [v[0] for v in out], [v[1] for v in out]


def swap_quarters(vs, lane):
    low64 = lane < 64
    low32 = lax.rem(lane, 64) < 32

    def roll(x, by):
        return pltpu.roll(x, by, 1)

    a0 = jnp.where(low64, vs[0], roll(vs[2], 64))
    a2 = jnp.where(low64, roll(vs[0], 64), vs[2])
    a1 = jnp.where(low64, vs[1], roll(vs[3], 64))
    a3 = jnp.where(low64, roll(vs[1], 64), vs[3])
    return [
        jnp.where(low32, a0, roll(a1, 32)),
        jnp.where(low32, roll(a0, 96), a1),
        jnp.where(low32, a2, roll(a3, 32)),
        jnp.where(low32, roll(a2, 96), a3),
    ]


def kernel(
    groups, rows, field_ref, index_ref, loss_ref, high_hbm, low_hbm, out_ref,
    high_ref, low_ref, term, total, coef, damp, edge, lhs, mid, field_halo, spec_send, spec_halo,
    b_send, b_recv, c_send, c_recv, d_send, d_recv,
    load_sem, halo_send_sem, halo_recv_sem, b_sems, c_sems, d_sems,
):
    depth = lax.axis_index("depth")
    me = lax.axis_index("rows")
    ahead = lax.rem(depth + 1, groups)
    behind = lax.rem(depth + groups - 1, groups)
    right, left = lax.rem(me + 1, rows), lax.rem(me + rows - 1, rows)
    tiles = high_ref.shape[0]
    slab = field_ref.shape[2]
    tall = slab + 2 * HALO

    loads = [
        pltpu.make_async_copy(high_hbm, high_ref, load_sem.at[0]),
        pltpu.make_async_copy(low_hbm, low_ref, load_sem.at[1]),
    ]
    for load in loads:
        load.start()

    barrier = pltpu.get_barrier_semaphore()

    def greet(step, carry):
        pl.semaphore_signal(barrier, inc=1, device_id=(depth, lax.rem(me + step, rows)), device_id_type=MESH)
        return carry

    def greet_behind(step, carry):
        pl.semaphore_signal(barrier, inc=1, device_id=(behind, lax.rem(me + step, rows)), device_id_type=MESH)
        return carry

    lax.fori_loop(1, rows, greet, 0)
    lax.fori_loop(0, rows, greet_behind, 0)

    lane32 = lax.broadcasted_iota(jnp.int32, (32, LANES), 1)
    lane16 = lax.broadcasted_iota(jnp.int32, (16, LANES), 1)
    lane_tall = lax.broadcasted_iota(jnp.int32, (tall, LANES), 1)
    row_tall = lax.broadcasted_iota(jnp.int32, (tall, LANES), 0)
    outside = ((row_tall < HALO) & (me == 0)) | ((row_tall >= HALO + slab) & (me == rows - 1))
    lat = jnp.where(outside, 0.0, lateral)
    first_lane = lane_tall == 0
    last_lane = lane_tall == LANES - 1
    lat_slab = jnp.full((slab, LANES), lateral, jnp.float32)

    for slot in range(2):
        for part in range(2):
            for a in range(tiles):
                term[slot, part, a, 0:HALO] = jnp.zeros((HALO, LANES), jnp.float32)
                term[slot, part, a, tall + HALO : tall + 2 * HALO] = jnp.zeros((HALO, LANES), jnp.float32)

    def all_copies(src, dst, sems, to_depth, step):
        target = lax.rem(me + step, rows)
        return pltpu.make_async_remote_copy(
            src_ref=src.at[target], dst_ref=dst.at[me], send_sem=sems.at[0, step], recv_sem=sems.at[1, step],
            device_id=(to_depth, target), device_id_type=MESH,
        )

    def start_all(src, dst, sems, to_depth, first):
        def body(step, carry):
            all_copies(src, dst, sems, to_depth, step).start()
            return carry

        lax.fori_loop(first, rows, body, 0)

    def wait_recv_all(src, dst, sems, to_depth, first):
        def body(step, carry):
            source = lax.rem(me + rows - step, rows)
            pltpu.make_async_remote_copy(
                src_ref=src.at[source], dst_ref=dst.at[source], send_sem=sems.at[0, step], recv_sem=sems.at[1, step],
                device_id=(to_depth, source), device_id_type=MESH,
            ).wait_recv()
            return carry

        lax.fori_loop(first, rows, body, 0)

    def wait_send_all(src, dst, sems, to_depth, first):
        def body(step, carry):
            all_copies(src, dst, sems, to_depth, step).wait_send()
            return carry

        lax.fori_loop(first, rows, body, 0)

    def halo_copies(tick):
        copies = []
        for side, target in ((0, left), (1, right)):
            there = 1 - side
            copies.append(
                pltpu.make_async_remote_copy(
                    src_ref=edge.at[tick, side], dst_ref=field_halo.at[tick, there],
                    send_sem=halo_send_sem.at[tick, 0, side], recv_sem=halo_recv_sem.at[tick, 0, there],
                    device_id=(depth, target), device_id_type=MESH,
                )
            )
        return copies

    def spec_copies(tick):
        copies = []
        for side, target in ((0, left), (1, right)):
            there = 1 - side
            copies.append(
                pltpu.make_async_remote_copy(
                    src_ref=spec_send.at[tick, side], dst_ref=spec_halo.at[tick, there],
                    send_sem=halo_send_sem.at[tick, 1, side], recv_sem=halo_recv_sem.at[tick, 1, there],
                    device_id=(depth, target), device_id_type=MESH,
                )
            )
        return copies

    def put_field(tick, part, a, value):
        term[0, part, a, 2 * HALO : 2 * HALO + slab] = value
        edge[tick, 0, part, a] = value[:HALO]
        edge[tick, 1, part, a] = value[slab - HALO :]

    def put_specimen(tick, a, values):
        for k in range(SLICES):
            coef[tick, k, a, HALO : HALO + slab] = contrast * values[k] - 4.0 * lat_slab
            damp[tick, k, a, HALO : HALO + slab] = contrast * values[SLICES + k]
        for kind in range(2):
            first, second = values[SLICES * kind], values[SLICES * kind + 1]
            top = jnp.concatenate([first[:HALO], second[:HALO]], axis=0)
            bottom = jnp.concatenate([first[slab - HALO :], second[slab - HALO :]], axis=0)
            spec_send[tick, 0, kind, a] = top.astype(jnp.bfloat16)
            spec_send[tick, 1, kind, a] = bottom.astype(jnp.bfloat16)

    def use_halos(tick):
        for copy in halo_copies(tick):
            copy.wait_recv()
        for copy in spec_copies(tick):
            copy.wait_recv()
        for side, start in ((0, 0), (1, HALO + slab)):
            off = (me == 0) if side == 0 else (me == rows - 1)
            keep = jnp.where(off, 0.0, 1.0)
            lat_here = lateral * keep
            for a in range(tiles):
                for part in range(2):
                    term[0, part, a, HALO + start : 2 * HALO + start] = field_halo[tick, side, part, a] * keep
                index = spec_halo[tick, side, 0, a].astype(jnp.float32)
                loss = spec_halo[tick, side, 1, a].astype(jnp.float32)
                for k in range(SLICES):
                    here = slice(k * HALO, (k + 1) * HALO)
                    coef[tick, k, a, start : start + HALO] = contrast * index[here] - 4.0 * lat_here
                    damp[tick, k, a, start : start + HALO] = contrast * loss[here]

    def one_term(tick, k, degree):
        src, dst = (degree - 1) % 2, degree % 2
        scale = 1.0 / degree
        lo, hi = HALO, HALO + tall
        centre, ahead_of, back_of = [], [], []
        for part in range(2):
            x = [term[src, part, a, lo:hi] for a in range(tiles)]
            centre.append(x)
            ahead_of.append([pltpu.roll(v, 1, 1) for v in x])
            back_of.append([pltpu.roll(v, LANES - 1, 1) for v in x])
        zero = jnp.zeros((tall, LANES), jnp.float32)
        for a in range(tiles):
            stirred = []
            for part in range(2):
                before = ahead_of[part][a - 1] if a > 0 else zero
                after = back_of[part][a + 1] if a < tiles - 1 else zero
                west = jnp.where(first_lane, before, ahead_of[part][a])
                east = jnp.where(last_lane, after, back_of[part][a])
                around = (term[src, part, a, lo - 1 : hi - 1] + term[src, part, a, lo + 1 : hi + 1]) + (west + east)
                stirred.append(lat * around + coef[tick, k, a] * centre[part][a])
            loss = damp[tick, k, a]
            new = [
                (-stirred[1] - loss * centre[0][a]) * scale,
                (stirred[0] - loss * centre[1][a]) * scale,
            ]
            for part in range(2):
                so_far = centre[part][a] if degree == 1 else total[part, a]
                if degree < TAYLOR:
                    term[dst, part, a, lo:hi] = new[part]
                    total[part, a] = so_far + new[part]
                else:
                    term[dst, part, a, lo:hi] = so_far + new[part]

    def march(tick):
        for k in range(SLICES):
            for degree in range(1, TAYLOR + 1):
                one_term(tick, k, degree)

    def convolve(load, store):
        for chunk in range(0, slab, 16):
            re = [load(0, a, chunk, 16) for a in range(tiles)]
            im = [load(1, a, chunk, 16) for a in range(tiles)]
            re, im = radix8(re, im, -1)
            for k1 in range(tiles):
                for part, value in ((0, re[k1]), (1, im[k1])):
                    at = slice(part * LANES, (part + 1) * LANES)
                    top = value.astype(jnp.bfloat16)
                    lhs[k1, chunk : chunk + 16, at] = top
                    lhs[k1, slab + chunk : slab + chunk + 16, at] = (value - top.astype(jnp.float32)).astype(jnp.bfloat16)
        for k1 in range(tiles):
            both = jnp.dot(lhs[k1], high_ref[k1], preferred_element_type=jnp.float32)
            rest = jnp.dot(lhs[k1, :slab], low_ref[k1], preferred_element_type=jnp.float32)
            mid[k1] = both[:slab] + (both[slab:] + rest)
        for chunk in range(0, slab, 16):
            re = [mid[k1, chunk : chunk + 16, :LANES] for k1 in range(tiles)]
            im = [mid[k1, chunk : chunk + 16, LANES:] for k1 in range(tiles)]
            re, im = radix8(re, im, 1)
            for a in range(tiles):
                store(0, a, chunk, 16, re[a])
                store(1, a, chunk, 16, im[a])

    def load_term(part, a, start, size):
        return term[0, part, a, 2 * HALO + start : 2 * HALO + start + size]

    def store_total(part, a, start, size, value):
        total[part, a, start : start + size] = value

    def load_total(part, a, start, size):
        return total[part, a, start : start + size]

    def pack(send):
        low64 = lane16 < 64
        for a in range(0, tiles, 2):
            stack = jnp.concatenate(
                [total[0, a, :slab], total[1, a, :slab], total[0, a + 1, :slab], total[1, a + 1, :slab]], axis=0
            )
            turned = stack.T
            for j in range(4):
                upper = turned[32 * j : 32 * j + 16]
                lower = turned[32 * j + 16 : 32 * j + 32]
                send[4 * a + j] = jnp.where(low64, upper, pltpu.roll(lower, 64, 1))
                send[4 * (a + 1) + j] = jnp.where(low64, pltpu.roll(upper, 64, 1), lower)

    def unpack(recv):
        for t in range(tiles):
            outs = swap_quarters([recv[4 * t + u] for u in range(4)], lane16)
            for c_high in range(2):
                for part in range(2):
                    total[part, t, 16 * c_high : 16 * c_high + 16] = outs[2 * c_high + part]

    for a in range(tiles):
        at = slice(a * LANES, (a + 1) * LANES)
        for part in range(2):
            put_field(0, part, a, field_ref[0, part, :, at])
        values = [ref[k, :, at].astype(jnp.float32) for ref in (index_ref, loss_ref) for k in range(SLICES)]
        put_specimen(0, a, values)
        turned = jnp.concatenate(values, axis=0).T
        for j in range(4):
            b_send[4 * a + j] = turned[32 * j : 32 * j + 32].astype(jnp.bfloat16)

    pl.semaphore_wait(barrier, 2 * rows - 1)
    for copy in halo_copies(0):
        copy.start()
    for copy in spec_copies(0):
        copy.start()
    start_all(b_send, b_recv, b_sems, depth, 1)
    b_recv[me] = b_send[me]

    use_halos(0)
    march(0)
    for load in loads:
        load.wait()
    convolve(load_term, store_total)
    pack(c_send)
    start_all(c_send, c_recv, c_sems, ahead, 0)

    wait_recv_all(b_send, b_recv, b_sems, depth, 1)
    for t in range(tiles):
        outs = swap_quarters([b_recv[4 * t + u].astype(jnp.float32) for u in range(4)], lane32)
        put_specimen(1, t, outs)
    for copy in spec_copies(1):
        copy.start()

    wait_recv_all(c_send, c_recv, c_sems, behind, 0)
    unpack(c_recv)

    def store_field(part, a, start, size, value):
        term[0, part, a, 2 * HALO + start : 2 * HALO + start + size] = value
        if start == 0:
            edge[1, 0, part, a] = value[:HALO]
        if start + size == slab:
            edge[1, 1, part, a] = value[size - HALO :]

    convolve(load_total, store_field)
    for copy in halo_copies(1):
        copy.start()
    use_halos(1)
    march(1)
    convolve(load_term, store_total)
    pack(d_send)
    start_all(d_send, d_recv, d_sems, depth, 1)
    d_recv[me] = d_send[me]
    wait_recv_all(d_send, d_recv, d_sems, depth, 1)
    unpack(d_recv)

    def store_out(part, a, start, size, value):
        out_ref[0, part, start : start + size, a * LANES : (a + 1) * LANES] = value

    convolve(load_total, store_out)

    for tick in range(2):
        for copy in halo_copies(tick) + spec_copies(tick):
            copy.wait_send()
    wait_send_all(b_send, b_recv, b_sems, depth, 1)
    wait_send_all(c_send, c_recv, c_sems, ahead, 0)
    wait_send_all(d_send, d_recv, d_sems, depth, 1)


def solution(mesh):
    groups, rows = mesh.shape["depth"], mesh.shape["rows"]

    def local(in_flight, phase_index, absorption):
        _, parts, slab, length = in_flight.shape
        tiles = length // LANES
        tall = slab + 2 * HALO
        high, low = middle_matrices(length)
        f32, bf16 = jnp.float32, jnp.bfloat16
        vmem = pl.BlockSpec(memory_space=pltpu.VMEM)
        return pl.pallas_call(
            functools.partial(kernel, groups, rows),
            out_shape=jax.ShapeDtypeStruct(in_flight.shape, f32),
            in_specs=[vmem, vmem, vmem, pl.BlockSpec(memory_space=pl.ANY), pl.BlockSpec(memory_space=pl.ANY)],
            out_specs=vmem,
            scratch_shapes=[
                pltpu.VMEM(high.shape, bf16),
                pltpu.VMEM(low.shape, bf16),
                pltpu.VMEM((2, parts, tiles, tall + 2 * HALO, LANES), f32),
                pltpu.VMEM((parts, tiles, tall, LANES), f32),
                pltpu.VMEM((2, SLICES, tiles, tall, LANES), f32),
                pltpu.VMEM((2, SLICES, tiles, tall, LANES), f32),
                pltpu.VMEM((2, 2, parts, tiles, HALO, LANES), f32),
                pltpu.VMEM((tiles, 2 * slab, 2 * LANES), bf16),
                pltpu.VMEM((tiles, slab, 2 * LANES), f32),
                pltpu.VMEM((2, 2, parts, tiles, HALO, LANES), f32),
                pltpu.VMEM((2, 2, 2, tiles, 2 * HALO, LANES), bf16),
                pltpu.VMEM((2, 2, 2, tiles, 2 * HALO, LANES), bf16),
                pltpu.VMEM((rows, 32, LANES), bf16),
                pltpu.VMEM((rows, 32, LANES), bf16),
                pltpu.VMEM((rows, 16, LANES), f32),
                pltpu.VMEM((rows, 16, LANES), f32),
                pltpu.VMEM((rows, 16, LANES), f32),
                pltpu.VMEM((rows, 16, LANES), f32),
                pltpu.SemaphoreType.DMA((2,)),
                pltpu.SemaphoreType.DMA((2, 2, 2)),
                pltpu.SemaphoreType.DMA((2, 2, 2)),
                pltpu.SemaphoreType.DMA((2, rows)),
                pltpu.SemaphoreType.DMA((2, rows)),
                pltpu.SemaphoreType.DMA((2, rows)),
            ],
            compiler_params=pltpu.CompilerParams(
                collective_id=0, has_side_effects=True, vmem_limit_bytes=32 * 1024 * 1024
            ),
        )(in_flight, phase_index, absorption, jnp.asarray(high), jnp.asarray(low))

    placed = (P("depth", None, "rows", None), P("depth", "rows", None), P("depth", "rows", None))
    return jax.shard_map(
        local, mesh=mesh, in_specs=placed, out_specs=P("depth", None, "rows", None), check_vma=False
    )
```

```python
import functools
import math

import jax
import jax.numpy as jnp
import ml_dtypes
import numpy as np
from jax import lax
from jax.experimental import pallas as pl
from jax.experimental.pallas import tpu as pltpu
from jax.sharding import PartitionSpec as P

TAYLOR = 4
SLICES = 2
HALO = 8
CHUNK = 16
PLANE_WIDTH = 4
LANES = 128
lateral = 0.22
contrast = 0.2
MESH = pl.DeviceIdType.MESH


def middle_matrices(length):
    coarse = length // LANES
    b = np.arange(LANES)
    k = np.arange(length)
    f = np.where(k < length // 2, k, k - length)
    gain = np.exp(-1j * np.pi * ((f * f) % (8 * length)) / (4 * length))
    dft = np.exp(-2j * np.pi * (np.outer(b, b) % LANES) / LANES)
    whole = np.zeros((coarse, 2 * LANES, 2 * LANES))
    for k1 in range(coarse):
        twiddle = np.exp(-2j * np.pi * b * k1 / length)
        m = (twiddle[:, None] * dft * gain[k1 + coarse * b][None, :]) @ (np.conj(dft) * np.conj(twiddle)[None, :])
        m = m / length
        whole[k1] = np.block([[m.real, m.imag], [-m.imag, m.real]])
    high = whole.astype(np.float32).astype(ml_dtypes.bfloat16)
    low = (whole - high.astype(np.float64)).astype(np.float32).astype(ml_dtypes.bfloat16)
    return high, low


def radix8(re, im, sign):
    half = math.sqrt(0.5)

    def turn(r, i):
        return (-i, r) if sign > 0 else (i, -r)

    def four(r, i):
        a, b = (r[0] + r[2], i[0] + i[2]), (r[0] - r[2], i[0] - i[2])
        c, d = (r[1] + r[3], i[1] + i[3]), (r[1] - r[3], i[1] - i[3])
        d = turn(*d)
        return [(a[0] + c[0], a[1] + c[1]), (b[0] + d[0], b[1] + d[1]), (a[0] - c[0], a[1] - c[1]), (b[0] - d[0], b[1] - d[1])]

    even = four(re[0::2], im[0::2])
    odd = four(re[1::2], im[1::2])
    s = 1.0 if sign > 0 else -1.0
    o1, o3 = odd[1], odd[3]
    odd[1] = ((o1[0] - s * o1[1]) * half, (o1[1] + s * o1[0]) * half)
    odd[2] = turn(*odd[2])
    odd[3] = ((-o3[0] - s * o3[1]) * half, (-o3[1] + s * o3[0]) * half)
    out = [(e[0] + o[0], e[1] + o[1]) for e, o in zip(even, odd)]
    out += [(e[0] - o[0], e[1] - o[1]) for e, o in zip(even, odd)]
    return [v[0] for v in out], [v[1] for v in out]


def far_first(height, width):
    def centred(v, n):
        return v if v <= n // 2 else v - n

    left = [(centred(y, height), centred(x, width)) for y in range(height) for x in range(width) if y or x]
    left.sort(key=lambda t: -(abs(t[0]) + abs(t[1])))
    order = []
    while left:
        t = left.pop(0)
        order.append(t)
        opposite = [u for u in left if (u[0] + t[0]) % height == 0 and (u[1] + t[1]) % width == 0]
        if opposite:
            left.remove(opposite[0])
            order.append(opposite[0])
    return order


def swap_quarters(vs, lane):
    low64 = lane < 64
    low32 = lax.rem(lane, 64) < 32

    def roll(x, by):
        return pltpu.roll(x, by, 1)

    a0 = jnp.where(low64, vs[0], roll(vs[2], 64))
    a2 = jnp.where(low64, roll(vs[0], 64), vs[2])
    a1 = jnp.where(low64, vs[1], roll(vs[3], 64))
    a3 = jnp.where(low64, roll(vs[1], 64), vs[3])
    return [
        jnp.where(low32, a0, roll(a1, 32)),
        jnp.where(low32, roll(a0, 96), a1),
        jnp.where(low32, a2, roll(a3, 32)),
        jnp.where(low32, roll(a2, 96), a3),
    ]


def kernel(
    groups, rows, width, field_hbm, index_hbm, loss_hbm, high_hbm, low_hbm, out_ref,
    field_ref, index_ref, loss_ref, high_ref, low_ref, term, total, coef, damp, edge, lhs, mid,
    first_field_halo, first_spec_halo, field_halo, spec_send, spec_halo,
    b_send, b_recv, c_send, c_recv, d_send, d_recv,
    load_sem, first_sems, halo_sems, b_sems, c_sems, d_sems,
):
    depth = lax.axis_index("depth")
    me = lax.axis_index("rows")
    ahead = lax.rem(depth + 1, groups)
    behind = lax.rem(depth + groups - 1, groups)
    right, left = lax.rem(me + 1, rows), lax.rem(me + rows - 1, rows)
    tiles = high_ref.shape[0]
    slab = field_ref.shape[2]
    tall = slab + 2 * HALO

    barrier = pltpu.get_barrier_semaphore()

    def greet(step, carry):
        pl.semaphore_signal(barrier, inc=1, device_id=(depth, lax.rem(me + step, rows)), device_id_type=MESH)
        return carry

    def greet_behind(step, carry):
        pl.semaphore_signal(barrier, inc=1, device_id=(behind, lax.rem(me + step, rows)), device_id_type=MESH)
        return carry

    lax.fori_loop(1, rows, greet, 0)
    lax.fori_loop(0, rows, greet_behind, 0)

    pairs = ((field_hbm, field_ref), (index_hbm, index_ref), (loss_hbm, loss_ref), (high_hbm, high_ref), (low_hbm, low_ref))
    loads = [pltpu.make_async_copy(src, dst, load_sem.at[i]) for i, (src, dst) in enumerate(pairs)]
    for load in loads:
        load.start()

    lane32 = lax.broadcasted_iota(jnp.int32, (32, LANES), 1)
    lane16 = lax.broadcasted_iota(jnp.int32, (16, LANES), 1)
    row_tall = lax.broadcasted_iota(jnp.int32, (tall, LANES), 0)
    outside = ((row_tall < HALO) & (me == 0)) | ((row_tall >= HALO + slab) & (me == rows - 1))
    lat = jnp.where(outside, 0.0, lateral)
    lat_slab = jnp.full((slab, LANES), lateral, jnp.float32)

    for slot in range(2):
        for part in range(2):
            for a in range(tiles):
                term[slot, part, a, 0:HALO] = jnp.zeros((HALO, LANES), jnp.float32)
                term[slot, part, a, tall + HALO : tall + 2 * HALO] = jnp.zeros((HALO, LANES), jnp.float32)

    own_y, own_x = me // width, lax.rem(me, width)
    height = rows // width
    order = far_first(height, width)

    def start_all(src, dst, sems, to_depth, with_self):
        for dy, dx in order + ([(0, 0)] if with_self else []):
            target = lax.rem(own_y + (dy + height), height) * width + lax.rem(own_x + (dx + width), width)
            pltpu.make_async_remote_copy(
                src_ref=src.at[target], dst_ref=dst.at[me], send_sem=sems.at[0], recv_sem=sems.at[1],
                device_id=(to_depth, target), device_id_type=MESH,
            ).start()

    def whole(src, dst, sems, with_self):
        count = rows if with_self else rows - 1
        return pltpu.make_async_remote_copy(
            src_ref=src.at[pl.ds(0, count)], dst_ref=dst.at[pl.ds(0, count)], send_sem=sems.at[0], recv_sem=sems.at[1],
            device_id=(depth, right), device_id_type=MESH,
        )

    def first_halo_copies():
        copies = []
        for side, target in ((0, left), (1, right)):
            there = 1 - side
            here = pl.ds(0 if side == 0 else slab - HALO, HALO)
            triples = (
                (field_hbm.at[0, :, here, :], first_field_halo.at[there]),
                (index_hbm.at[:, here, :], first_spec_halo.at[there, 0]),
                (loss_hbm.at[:, here, :], first_spec_halo.at[there, 1]),
            )
            for n, (src, dst) in enumerate(triples):
                copies.append(
                    pltpu.make_async_remote_copy(
                        src_ref=src, dst_ref=dst,
                        send_sem=first_sems.at[0, n, side], recv_sem=first_sems.at[1, n, there],
                        device_id=(depth, target), device_id_type=MESH,
                    )
                )
        return copies

    def halo_copies(src, dst, kind):
        copies = []
        for side, target in ((0, left), (1, right)):
            there = 1 - side
            copies.append(
                pltpu.make_async_remote_copy(
                    src_ref=src.at[side], dst_ref=dst.at[there],
                    send_sem=halo_sems.at[0, kind, side], recv_sem=halo_sems.at[1, kind, there],
                    device_id=(depth, target), device_id_type=MESH,
                )
            )
        return copies

    def put_coefficients(tick, a, values):
        for k in range(SLICES):
            coef[tick, k, a, HALO : HALO + slab] = contrast * values[k] - 4.0 * lat_slab
            damp[tick, k, a, HALO : HALO + slab] = contrast * values[SLICES + k]

    def put_spec_edges(a, values):
        for kind in range(2):
            first, second = values[SLICES * kind], values[SLICES * kind + 1]
            top = jnp.concatenate([first[:HALO], second[:HALO]], axis=0)
            bottom = jnp.concatenate([first[slab - HALO :], second[slab - HALO :]], axis=0)
            spec_send[0, kind, a] = top.astype(jnp.bfloat16)
            spec_send[1, kind, a] = bottom.astype(jnp.bfloat16)

    def use_halos(tick, field_of, spec_of):
        for side, start in ((0, 0), (1, HALO + slab)):
            off = (me == 0) if side == 0 else (me == rows - 1)
            keep = jnp.where(off, 0.0, 1.0)
            lat_here = lateral * keep
            for a in range(tiles):
                for part in range(2):
                    term[0, part, a, HALO + start : 2 * HALO + start] = field_of(side, part, a) * keep
                for k in range(SLICES):
                    coef[tick, k, a, start : start + HALO] = contrast * spec_of(side, 0, k, a) - 4.0 * lat_here
                    damp[tick, k, a, start : start + HALO] = contrast * spec_of(side, 1, k, a)

    lane_chunk = lax.broadcasted_iota(jnp.int32, (CHUNK, LANES), 1)
    first_lane = lane_chunk == 0
    last_lane = lane_chunk == LANES - 1
    nothing = jnp.zeros((CHUNK, LANES), jnp.float32)

    def one_term(tick, k, degree):
        src, dst = (degree - 1) % 2, degree % 2
        scale = 1.0 / degree
        final = k == SLICES - 1 and degree == TAYLOR
        for r in range(HALO if final else 0, HALO + slab if final else tall, CHUNK):
            at = slice(r, r + CHUNK)
            lo, hi = HALO + r, HALO + r + CHUNK

            def fetch(a):
                if a < 0 or a >= tiles:
                    return [(nothing, nothing, nothing)] * 2
                xs = [term[src, part, a, lo:hi] for part in range(2)]
                return [(x, pltpu.roll(x, 1, 1), pltpu.roll(x, LANES - 1, 1)) for x in xs]

            before, here = fetch(-1), fetch(0)
            for a in range(tiles):
                after = fetch(a + 1)
                stirred = []
                for part in range(2):
                    west = jnp.where(first_lane, before[part][1], here[part][1])
                    east = jnp.where(last_lane, after[part][2], here[part][2])
                    beside = term[src, part, a, lo - 1 : hi - 1] + term[src, part, a, lo + 1 : hi + 1]
                    stirred.append(lat[at] * (beside + (west + east)) + coef[tick, k, a, at] * here[part][0])
                loss = damp[tick, k, a, at]
                new = [
                    (stirred[1] + loss * here[0][0]) * (-scale),
                    (stirred[0] - loss * here[1][0]) * scale,
                ]
                for part in range(2):
                    so_far = here[part][0] if degree == 1 else total[part, a, at]
                    if degree < TAYLOR:
                        term[dst, part, a, lo:hi] = new[part]
                        total[part, a, at] = so_far + new[part]
                    else:
                        term[dst, part, a, lo:hi] = so_far + new[part]
                before, here = here, after

    def march(tick):
        for k in range(SLICES):
            for degree in range(1, TAYLOR + 1):
                one_term(tick, k, degree)

    def convolve(load, store):
        for chunk in range(0, slab, 16):
            re = [load(0, a, chunk, 16) for a in range(tiles)]
            im = [load(1, a, chunk, 16) for a in range(tiles)]
            re, im = radix8(re, im, -1)
            for k1 in range(tiles):
                for part, value in ((0, re[k1]), (1, im[k1])):
                    at = slice(part * LANES, (part + 1) * LANES)
                    top = value.astype(jnp.bfloat16)
                    lhs[k1, chunk : chunk + 16, at] = top
                    lhs[k1, slab + chunk : slab + chunk + 16, at] = (value - top.astype(jnp.float32)).astype(jnp.bfloat16)
        for k1 in range(tiles):
            both = jnp.dot(lhs[k1], high_ref[k1], preferred_element_type=jnp.float32)
            rest = jnp.dot(lhs[k1, :slab], low_ref[k1], preferred_element_type=jnp.float32)
            mid[k1] = both[:slab] + (both[slab:] + rest)
        for chunk in range(0, slab, 16):
            re = [mid[k1, chunk : chunk + 16, :LANES] for k1 in range(tiles)]
            im = [mid[k1, chunk : chunk + 16, LANES:] for k1 in range(tiles)]
            re, im = radix8(re, im, 1)
            for a in range(tiles):
                store(0, a, chunk, 16, re[a])
                store(1, a, chunk, 16, im[a])

    def load_term(part, a, start, size):
        return term[0, part, a, 2 * HALO + start : 2 * HALO + start + size]

    def store_total(part, a, start, size, value):
        total[part, a, start : start + size] = value

    def load_total(part, a, start, size):
        return total[part, a, start : start + size]

    def pack(send):
        low64 = lane16 < 64
        for a in range(0, tiles, 2):
            stack = jnp.concatenate(
                [total[0, a, :slab], total[1, a, :slab], total[0, a + 1, :slab], total[1, a + 1, :slab]], axis=0
            )
            turned = stack.T
            for j in range(4):
                upper = turned[32 * j : 32 * j + 16]
                lower = turned[32 * j + 16 : 32 * j + 32]
                send[4 * a + j] = jnp.where(low64, upper, pltpu.roll(lower, 64, 1))
                send[4 * (a + 1) + j] = jnp.where(low64, pltpu.roll(upper, 64, 1), lower)

    def unpack(recv):
        for t in range(tiles):
            outs = swap_quarters([recv[4 * t + u] for u in range(4)], lane16)
            for c_high in range(2):
                for part in range(2):
                    total[part, t, 16 * c_high : 16 * c_high + 16] = outs[2 * c_high + part]

    pl.semaphore_wait(barrier, 2 * rows - 1)
    for copy in first_halo_copies():
        copy.start()

    for load in loads[:3]:
        load.wait()
    for a in range(tiles):
        at = slice(a * LANES, (a + 1) * LANES)
        for part in range(2):
            term[0, part, a, 2 * HALO : 2 * HALO + slab] = field_ref[0, part, :, at]
        values = [ref[k, :, at].astype(jnp.float32) for ref in (index_ref, loss_ref) for k in range(SLICES)]
        put_coefficients(0, a, values)
        turned = jnp.concatenate(values, axis=0).T
        for j in range(4):
            b_send[4 * a + j] = turned[32 * j : 32 * j + 32].astype(jnp.bfloat16)
    start_all(b_send, b_recv, b_sems, depth, False)
    b_recv[me] = b_send[me]

    for copy in first_halo_copies():
        copy.wait_recv()
    use_halos(
        0,
        lambda side, part, a: first_field_halo[side, part, :, a * LANES : (a + 1) * LANES],
        lambda side, kind, k, a: first_spec_halo[side, kind, k, :, a * LANES : (a + 1) * LANES].astype(jnp.float32),
    )
    march(0)
    for load in loads[3:]:
        load.wait()
    convolve(load_term, store_total)
    pack(c_send)
    start_all(c_send, c_recv, c_sems, ahead, True)

    whole(b_send, b_recv, b_sems, False).wait_recv()
    for t in range(tiles):
        outs = swap_quarters([b_recv[4 * t + u].astype(jnp.float32) for u in range(4)], lane32)
        put_coefficients(1, t, outs)
        put_spec_edges(t, outs)
    spec_copies = halo_copies(spec_send, spec_halo, 1)
    for copy in spec_copies:
        copy.start()

    whole(c_send, c_recv, c_sems, True).wait_recv()
    unpack(c_recv)

    def store_field(part, a, start, size, value):
        term[0, part, a, 2 * HALO + start : 2 * HALO + start + size] = value
        if start == 0:
            edge[0, part, a] = value[:HALO]
        if start + size == slab:
            edge[1, part, a] = value[size - HALO :]

    convolve(load_total, store_field)
    field_copies = halo_copies(edge, field_halo, 0)
    for copy in field_copies:
        copy.start()
    for copy in field_copies + spec_copies:
        copy.wait_recv()
    use_halos(
        1,
        lambda side, part, a: field_halo[side, part, a],
        lambda side, kind, k, a: spec_halo[side, kind, a].astype(jnp.float32)[k * HALO : (k + 1) * HALO],
    )
    march(1)
    convolve(load_term, store_total)
    pack(d_send)
    start_all(d_send, d_recv, d_sems, depth, False)
    d_recv[me] = d_send[me]
    whole(d_send, d_recv, d_sems, False).wait_recv()
    unpack(d_recv)

    def store_out(part, a, start, size, value):
        out_ref[0, part, start : start + size, a * LANES : (a + 1) * LANES] = value

    convolve(load_total, store_out)

    for copy in first_halo_copies() + spec_copies + field_copies:
        copy.wait_send()
    whole(b_send, b_recv, b_sems, False).wait_send()
    whole(c_send, c_recv, c_sems, True).wait_send()
    whole(d_send, d_recv, d_sems, False).wait_send()


def solution(mesh):
    groups, rows = mesh.shape["depth"], mesh.shape["rows"]

    def local(in_flight, phase_index, absorption):
        _, parts, slab, length = in_flight.shape
        tiles = length // LANES
        tall = slab + 2 * HALO
        high, low = middle_matrices(length)
        f32, bf16 = jnp.float32, jnp.bfloat16
        vmem = pl.BlockSpec(memory_space=pltpu.VMEM)
        return pl.pallas_call(
            functools.partial(kernel, groups, rows, PLANE_WIDTH),
            out_shape=jax.ShapeDtypeStruct(in_flight.shape, f32),
            in_specs=[pl.BlockSpec(memory_space=pltpu.HBM)] * 5,
            out_specs=vmem,
            scratch_shapes=[
                pltpu.VMEM(in_flight.shape, f32),
                pltpu.VMEM(phase_index.shape, bf16),
                pltpu.VMEM(absorption.shape, bf16),
                pltpu.VMEM(high.shape, bf16),
                pltpu.VMEM(low.shape, bf16),
                pltpu.VMEM((2, parts, tiles, tall + 2 * HALO, LANES), f32),
                pltpu.VMEM((parts, tiles, tall, LANES), f32),
                pltpu.VMEM((2, SLICES, tiles, tall, LANES), f32),
                pltpu.VMEM((2, SLICES, tiles, tall, LANES), f32),
                pltpu.VMEM((2, parts, tiles, HALO, LANES), f32),
                pltpu.VMEM((tiles, 2 * slab, 2 * LANES), bf16),
                pltpu.VMEM((tiles, slab, 2 * LANES), f32),
                pltpu.VMEM((2, parts, HALO, length), f32),
                pltpu.VMEM((2, 2, SLICES, HALO, length), bf16),
                pltpu.VMEM((2, parts, tiles, HALO, LANES), f32),
                pltpu.VMEM((2, 2, tiles, 2 * HALO, LANES), bf16),
                pltpu.VMEM((2, 2, tiles, 2 * HALO, LANES), bf16),
                pltpu.VMEM((rows, 32, LANES), bf16),
                pltpu.VMEM((rows, 32, LANES), bf16),
                pltpu.VMEM((rows, 16, LANES), f32),
                pltpu.VMEM((rows, 16, LANES), f32),
                pltpu.VMEM((rows, 16, LANES), f32),
                pltpu.VMEM((rows, 16, LANES), f32),
                pltpu.SemaphoreType.DMA((5,)),
                pltpu.SemaphoreType.DMA((2, 3, 2)),
                pltpu.SemaphoreType.DMA((2, 2, 2)),
                pltpu.SemaphoreType.DMA((2,)),
                pltpu.SemaphoreType.DMA((2,)),
                pltpu.SemaphoreType.DMA((2,)),
            ],
            compiler_params=pltpu.CompilerParams(
                collective_id=0, has_side_effects=True, vmem_limit_bytes=60 * 1024 * 1024
            ),
        )(in_flight, phase_index, absorption, jnp.asarray(high), jnp.asarray(low))

    placed = (P("depth", None, "rows", None), P("depth", "rows", None), P("depth", "rows", None))
    return jax.shard_map(
        local, mesh=mesh, in_specs=placed, out_specs=P("depth", None, "rows", None), check_vma=False
    )
```

```python
import functools
import math

import jax
import jax.numpy as jnp
import ml_dtypes
import numpy as np
from jax import lax
from jax.experimental import pallas as pl
from jax.experimental.pallas import tpu as pltpu
from jax.sharding import PartitionSpec as P

TAYLOR = 4
SLICES = 2
HALO = 8
CHUNK = 16
PLANE_WIDTH = 4
LANES = 128
lateral = 0.22
contrast = 0.2
MESH = pl.DeviceIdType.MESH


def middle_matrices(length):
    coarse = length // LANES
    b = np.arange(LANES)
    k = np.arange(length)
    f = np.where(k < length // 2, k, k - length)
    gain = np.exp(-1j * np.pi * ((f * f) % (8 * length)) / (4 * length))
    dft = np.exp(-2j * np.pi * (np.outer(b, b) % LANES) / LANES)
    whole = np.zeros((coarse, 2 * LANES, 2 * LANES))
    for k1 in range(coarse):
        twiddle = np.exp(-2j * np.pi * b * k1 / length)
        m = (twiddle[:, None] * dft * gain[k1 + coarse * b][None, :]) @ (np.conj(dft) * np.conj(twiddle)[None, :])
        m = m / length
        whole[k1] = np.block([[m.real, m.imag], [-m.imag, m.real]])
    high = whole.astype(np.float32).astype(ml_dtypes.bfloat16)
    low = (whole - high.astype(np.float64)).astype(np.float32).astype(ml_dtypes.bfloat16)
    return high, low


def radix8(re, im, sign):
    half = math.sqrt(0.5)

    def turn(r, i):
        return (-i, r) if sign > 0 else (i, -r)

    def four(r, i):
        a, b = (r[0] + r[2], i[0] + i[2]), (r[0] - r[2], i[0] - i[2])
        c, d = (r[1] + r[3], i[1] + i[3]), (r[1] - r[3], i[1] - i[3])
        d = turn(*d)
        return [(a[0] + c[0], a[1] + c[1]), (b[0] + d[0], b[1] + d[1]), (a[0] - c[0], a[1] - c[1]), (b[0] - d[0], b[1] - d[1])]

    even = four(re[0::2], im[0::2])
    odd = four(re[1::2], im[1::2])
    s = 1.0 if sign > 0 else -1.0
    o1, o3 = odd[1], odd[3]
    odd[1] = ((o1[0] - s * o1[1]) * half, (o1[1] + s * o1[0]) * half)
    odd[2] = turn(*odd[2])
    odd[3] = ((-o3[0] - s * o3[1]) * half, (-o3[1] + s * o3[0]) * half)
    out = [(e[0] + o[0], e[1] + o[1]) for e, o in zip(even, odd)]
    out += [(e[0] - o[0], e[1] - o[1]) for e, o in zip(even, odd)]
    return [v[0] for v in out], [v[1] for v in out]


def far_first(height, width):
    def centred(v, n):
        return v if v <= n // 2 else v - n

    left = [(centred(y, height), centred(x, width)) for y in range(height) for x in range(width) if y or x]
    left.sort(key=lambda t: -(abs(t[0]) + abs(t[1])))
    order = []
    while left:
        t = left.pop(0)
        order.append(t)
        opposite = [u for u in left if (u[0] + t[0]) % height == 0 and (u[1] + t[1]) % width == 0]
        if opposite:
            left.remove(opposite[0])
            order.append(opposite[0])
    return order


def swap_quarters(vs, lane):
    low64 = lane < 64
    low32 = lax.rem(lane, 64) < 32

    def roll(x, by):
        return pltpu.roll(x, by, 1)

    a0 = jnp.where(low64, vs[0], roll(vs[2], 64))
    a2 = jnp.where(low64, roll(vs[0], 64), vs[2])
    a1 = jnp.where(low64, vs[1], roll(vs[3], 64))
    a3 = jnp.where(low64, roll(vs[1], 64), vs[3])
    return [
        jnp.where(low32, a0, roll(a1, 32)),
        jnp.where(low32, roll(a0, 96), a1),
        jnp.where(low32, a2, roll(a3, 32)),
        jnp.where(low32, roll(a2, 96), a3),
    ]


def kernel(
    groups, rows, width, field_hbm, index_hbm, loss_hbm, high_hbm, low_hbm, out_ref,
    field_ref, index_ref, loss_ref, high_ref, low_ref, term, total, coef, damp, lhs, mid,
    first_field_halo, first_spec_halo, spec_send, spec_halo,
    b_send, b_recv, c_send, c_recv, d_send, d_recv,
    load_sem, first_sems, halo_sems, b_sems, c_sems, d_sems,
):
    depth = lax.axis_index("depth")
    me = lax.axis_index("rows")
    ahead = lax.rem(depth + 1, groups)
    behind = lax.rem(depth + groups - 1, groups)
    right, left = lax.rem(me + 1, rows), lax.rem(me + rows - 1, rows)
    tiles = high_ref.shape[0]
    slab = field_ref.shape[2]
    tall = slab + 2 * HALO

    barrier = pltpu.get_barrier_semaphore()

    def greet(step, carry):
        pl.semaphore_signal(barrier, inc=1, device_id=(depth, lax.rem(me + step, rows)), device_id_type=MESH)
        return carry

    def greet_behind(step, carry):
        pl.semaphore_signal(barrier, inc=1, device_id=(behind, lax.rem(me + step, rows)), device_id_type=MESH)
        return carry

    lax.fori_loop(1, rows, greet, 0)
    pairs = ((field_hbm, field_ref), (index_hbm, index_ref), (loss_hbm, loss_ref), (high_hbm, high_ref), (low_hbm, low_ref))
    loads = [pltpu.make_async_copy(src, dst, load_sem.at[i]) for i, (src, dst) in enumerate(pairs)]
    for load in loads:
        load.start()
    lax.fori_loop(0, rows, greet_behind, 0)

    lane32 = lax.broadcasted_iota(jnp.int32, (32, LANES), 1)
    lane8 = lax.broadcasted_iota(jnp.int32, (8, LANES), 1)
    lane16 = lax.broadcasted_iota(jnp.int32, (16, LANES), 1)
    row_tall = lax.broadcasted_iota(jnp.int32, (tall, LANES), 0)
    outside = ((row_tall < HALO) & (me == 0)) | ((row_tall >= HALO + slab) & (me == rows - 1))
    lat = jnp.where(outside, 0.0, lateral)
    lat_slab = jnp.full((slab, LANES), lateral, jnp.float32)

    for slot in range(2):
        for part in range(2):
            for a in range(tiles):
                term[slot, part, a, 0:HALO] = jnp.zeros((HALO, LANES), jnp.float32)
                term[slot, part, a, tall + HALO : tall + 2 * HALO] = jnp.zeros((HALO, LANES), jnp.float32)

    own_y, own_x = me // width, lax.rem(me, width)
    height = rows // width
    order = far_first(height, width)

    def start_all(src, dst, sems, to_depth, with_self):
        for dy, dx in order + ([(0, 0)] if with_self else []):
            target = lax.rem(own_y + (dy + height), height) * width + lax.rem(own_x + (dx + width), width)
            pltpu.make_async_remote_copy(
                src_ref=src.at[target], dst_ref=dst.at[me], send_sem=sems.at[0], recv_sem=sems.at[1],
                device_id=(to_depth, target), device_id_type=MESH,
            ).start()

    def whole(src, dst, sems, with_self):
        count = rows if with_self else rows - 1
        return pltpu.make_async_remote_copy(
            src_ref=src.at[pl.ds(0, count)], dst_ref=dst.at[pl.ds(0, count)], send_sem=sems.at[0], recv_sem=sems.at[1],
            device_id=(depth, right), device_id_type=MESH,
        )

    def first_halo_copies():
        copies = []
        for side, target in ((0, left), (1, right)):
            there = 1 - side
            here = pl.ds(0 if side == 0 else slab - HALO, HALO)
            triples = (
                (field_hbm.at[0, :, here, :], first_field_halo.at[there]),
                (index_hbm.at[:, here, :], first_spec_halo.at[there, 0]),
                (loss_hbm.at[:, here, :], first_spec_halo.at[there, 1]),
            )
            for n, (src, dst) in enumerate(triples):
                copies.append(
                    pltpu.make_async_remote_copy(
                        src_ref=src, dst_ref=dst,
                        send_sem=first_sems.at[0, n, side], recv_sem=first_sems.at[1, n, there],
                        device_id=(depth, target), device_id_type=MESH,
                    )
                )
        return copies

    def halo_copies(src, dst, kind):
        copies = []
        for side, target in ((0, left), (1, right)):
            there = 1 - side
            copies.append(
                pltpu.make_async_remote_copy(
                    src_ref=src.at[side], dst_ref=dst.at[there],
                    send_sem=halo_sems.at[0, kind, side], recv_sem=halo_sems.at[1, kind, there],
                    device_id=(depth, target), device_id_type=MESH,
                )
            )
        return copies

    def put_coefficients(tick, a, values):
        for k in range(SLICES):
            coef[tick, k, a, HALO : HALO + slab] = contrast * values[k] - 4.0 * lat_slab
            damp[tick, k, a, HALO : HALO + slab] = contrast * values[SLICES + k]

    def put_spec_edges(a, values):
        for kind in range(2):
            first, second = values[SLICES * kind], values[SLICES * kind + 1]
            top = jnp.concatenate([first[:HALO], second[:HALO]], axis=0)
            bottom = jnp.concatenate([first[slab - HALO :], second[slab - HALO :]], axis=0)
            spec_send[0, kind, a] = top.astype(jnp.bfloat16)
            spec_send[1, kind, a] = bottom.astype(jnp.bfloat16)

    def use_halos(tick, field_of, spec_of):
        for side, start in ((0, 0), (1, HALO + slab)):
            off = (me == 0) if side == 0 else (me == rows - 1)
            keep = jnp.where(off, 0.0, 1.0)
            lat_here = lateral * keep
            for a in range(tiles):
                for part in range(2) if field_of else ():
                    term[0, part, a, HALO + start : 2 * HALO + start] = field_of(side, part, a) * keep
                for k in range(SLICES):
                    coef[tick, k, a, start : start + HALO] = contrast * spec_of(side, 0, k, a) - 4.0 * lat_here
                    damp[tick, k, a, start : start + HALO] = contrast * spec_of(side, 1, k, a)

    lane_chunk = lax.broadcasted_iota(jnp.int32, (CHUNK, LANES), 1)
    first_lane = lane_chunk == 0
    last_lane = lane_chunk == LANES - 1
    nothing = jnp.zeros((CHUNK, LANES), jnp.float32)

    def one_term(tick, k, degree):
        src, dst = (degree - 1) % 2, degree % 2
        scale = 1.0 / degree
        final = k == SLICES - 1 and degree == TAYLOR
        for r in range(HALO if final else 0, HALO + slab if final else tall, CHUNK):
            at = slice(r, r + CHUNK)
            lo, hi = HALO + r, HALO + r + CHUNK

            def fetch(a):
                if a < 0 or a >= tiles:
                    return [(nothing, nothing, nothing)] * 2
                xs = [term[src, part, a, lo:hi] for part in range(2)]
                return [(x, pltpu.roll(x, 1, 1), pltpu.roll(x, LANES - 1, 1)) for x in xs]

            before, here = fetch(-1), fetch(0)
            for a in range(tiles):
                after = fetch(a + 1)
                stirred = []
                for part in range(2):
                    west = jnp.where(first_lane, before[part][1], here[part][1])
                    east = jnp.where(last_lane, after[part][2], here[part][2])
                    beside = term[src, part, a, lo - 1 : hi - 1] + term[src, part, a, lo + 1 : hi + 1]
                    stirred.append(lat[at] * (beside + (west + east)) + coef[tick, k, a, at] * here[part][0])
                loss = damp[tick, k, a, at]
                new = [
                    (stirred[1] + loss * here[0][0]) * (-scale),
                    (stirred[0] - loss * here[1][0]) * scale,
                ]
                for part in range(2):
                    so_far = here[part][0] if degree == 1 else total[part, a, at]
                    if degree < TAYLOR:
                        term[dst, part, a, lo:hi] = new[part]
                        total[part, a, at] = so_far + new[part]
                    else:
                        term[dst, part, a, lo:hi] = so_far + new[part]
                before, here = here, after

    def march(tick):
        for k in range(SLICES):
            for degree in range(1, TAYLOR + 1):
                one_term(tick, k, degree)

    def convolve(load, store, slab=slab):
        for chunk in range(0, slab, 16):
            re = [load(0, a, chunk, 16) for a in range(tiles)]
            im = [load(1, a, chunk, 16) for a in range(tiles)]
            re, im = radix8(re, im, -1)
            for k1 in range(tiles):
                for part, value in ((0, re[k1]), (1, im[k1])):
                    at = slice(part * LANES, (part + 1) * LANES)
                    top = value.astype(jnp.bfloat16)
                    lhs[k1, chunk : chunk + 16, at] = top
                    lhs[k1, slab + chunk : slab + chunk + 16, at] = (value - top.astype(jnp.float32)).astype(jnp.bfloat16)
        for k1 in range(tiles):
            both = jnp.dot(lhs[k1, : 2 * slab], high_ref[k1], preferred_element_type=jnp.float32)
            rest = jnp.dot(lhs[k1, :slab], low_ref[k1], preferred_element_type=jnp.float32)
            mid[k1, :slab] = both[:slab] + (both[slab:] + rest)
        for chunk in range(0, slab, 16):
            re = [mid[k1, chunk : chunk + 16, :LANES] for k1 in range(tiles)]
            im = [mid[k1, chunk : chunk + 16, LANES:] for k1 in range(tiles)]
            re, im = radix8(re, im, 1)
            for a in range(tiles):
                store(0, a, chunk, 16, re[a])
                store(1, a, chunk, 16, im[a])

    def load_term(part, a, start, size):
        return term[0, part, a, 2 * HALO + start : 2 * HALO + start + size]

    def store_total(part, a, start, size, value):
        total[part, a, start : start + size] = value

    def load_total(part, a, start, size):
        return total[part, a, start : start + size]

    def pack(send):
        low64 = lane16 < 64
        for a in range(0, tiles, 2):
            stack = jnp.concatenate(
                [total[0, a, :slab], total[1, a, :slab], total[0, a + 1, :slab], total[1, a + 1, :slab]], axis=0
            )
            turned = stack.T
            for j in range(4):
                upper = turned[32 * j : 32 * j + 16]
                lower = turned[32 * j + 16 : 32 * j + 32]
                send[4 * a + j, 0:16] = jnp.where(low64, upper, pltpu.roll(lower, 64, 1))
                send[4 * (a + 1) + j, 0:16] = jnp.where(low64, pltpu.roll(upper, 64, 1), lower)

    def unpack(recv, first):
        for t in range(tiles):
            outs = swap_quarters([recv[4 * t + u, 0:16] for u in range(4)], lane16)
            for c_high in range(2):
                for part in range(2):
                    at = first + 16 * c_high
                    total[part, t, at : at + 16] = outs[2 * c_high + part]

    def pack_halos(send):
        low = lane8 < 64
        for r in range(rows):
            joined = jnp.where(low, send[(r + 1) % rows, 0:8], send[(r + rows - 1) % rows, 8:16])
            send[r, 16:24] = pltpu.roll(joined, 64, 1)

    def unpack_halos(recv):
        keeps = [jnp.where(me == edge_at, 0.0, 1.0) for edge_at in (0, rows - 1)]
        for t in range(tiles):
            outs = swap_quarters([recv[4 * t + u, 16:24] for u in range(4)], lane8)
            for side, start in ((0, 0), (1, HALO + slab)):
                for part in range(2):
                    total[part, t, start : start + HALO] = outs[2 * side + part] * keeps[side]

    def specimen(a):
        at = slice(a * LANES, (a + 1) * LANES)
        return [ref[k, :, at].astype(jnp.float32) for ref in (index_ref, loss_ref) for k in range(SLICES)]

    def pack_specimen():
        for a in range(tiles):
            turned = jnp.concatenate(specimen(a), axis=0).T
            for j in range(4):
                b_send[4 * a + j] = turned[32 * j : 32 * j + 32].astype(jnp.bfloat16)
        b_recv[me] = b_send[me]

    def enter():
        pl.semaphore_wait(barrier, 2 * rows - 1)
        for copy in first_halo_copies():
            copy.start()

    for load in loads[1:3]:
        load.wait()
    pack_specimen()
    enter()
    start_all(b_send, b_recv, b_sems, depth, False)
    loads[0].wait()
    for a in range(tiles):
        for part in range(2):
            term[0, part, a, 2 * HALO : 2 * HALO + slab] = field_ref[0, part, :, a * LANES : (a + 1) * LANES]
        put_coefficients(0, a, specimen(a))

    for copy in first_halo_copies():
        copy.wait_recv()
    use_halos(
        0,
        lambda side, part, a: first_field_halo[side, part, :, a * LANES : (a + 1) * LANES],
        lambda side, kind, k, a: first_spec_halo[side, kind, k, :, a * LANES : (a + 1) * LANES].astype(jnp.float32),
    )
    march(0)
    for load in loads[3:]:
        load.wait()
    convolve(load_term, store_total)
    pack(c_send)
    pack_halos(c_send)
    start_all(c_send, c_recv, c_sems, ahead, True)

    whole(b_send, b_recv, b_sems, False).wait_recv()
    for t in range(tiles):
        outs = swap_quarters([b_recv[4 * t + u].astype(jnp.float32) for u in range(4)], lane32)
        put_coefficients(1, t, outs)
        put_spec_edges(t, outs)
    spec_copies = halo_copies(spec_send, spec_halo, 1)
    for copy in spec_copies:
        copy.start()

    whole(c_send, c_recv, c_sems, True).wait_recv()
    unpack(c_recv, HALO)
    unpack_halos(c_recv)

    def store_field(part, a, start, size, value):
        term[0, part, a, HALO + start : HALO + start + size] = value

    convolve(load_total, store_field, tall)
    for copy in spec_copies:
        copy.wait_recv()
    use_halos(
        1,
        None,
        lambda side, kind, k, a: spec_halo[side, kind, a].astype(jnp.float32)[k * HALO : (k + 1) * HALO],
    )
    march(1)
    convolve(load_term, store_total)
    pack(d_send)
    start_all(d_send, d_recv, d_sems, depth, False)
    d_recv[me] = d_send[me]
    whole(d_send, d_recv, d_sems, False).wait_recv()
    unpack(d_recv, 0)

    def store_out(part, a, start, size, value):
        out_ref[0, part, start : start + size, a * LANES : (a + 1) * LANES] = value

    convolve(load_total, store_out)

    for copy in first_halo_copies() + spec_copies:
        copy.wait_send()
    whole(b_send, b_recv, b_sems, False).wait_send()
    whole(c_send, c_recv, c_sems, True).wait_send()
    whole(d_send, d_recv, d_sems, False).wait_send()


def solution(mesh):
    groups, rows = mesh.shape["depth"], mesh.shape["rows"]

    def local(in_flight, phase_index, absorption):
        _, parts, slab, length = in_flight.shape
        tiles = length // LANES
        tall = slab + 2 * HALO
        high, low = middle_matrices(length)
        f32, bf16 = jnp.float32, jnp.bfloat16
        vmem = pl.BlockSpec(memory_space=pltpu.VMEM)
        return pl.pallas_call(
            functools.partial(kernel, groups, rows, PLANE_WIDTH),
            out_shape=jax.ShapeDtypeStruct(in_flight.shape, f32),
            in_specs=[pl.BlockSpec(memory_space=pltpu.HBM)] * 5,
            out_specs=vmem,
            scratch_shapes=[
                pltpu.VMEM(in_flight.shape, f32),
                pltpu.VMEM(phase_index.shape, bf16),
                pltpu.VMEM(absorption.shape, bf16),
                pltpu.VMEM(high.shape, bf16),
                pltpu.VMEM(low.shape, bf16),
                pltpu.VMEM((2, parts, tiles, tall + 2 * HALO, LANES), f32),
                pltpu.VMEM((parts, tiles, tall, LANES), f32),
                pltpu.VMEM((2, SLICES, tiles, tall, LANES), f32),
                pltpu.VMEM((2, SLICES, tiles, tall, LANES), f32),
                pltpu.VMEM((tiles, 2 * tall, 2 * LANES), bf16),
                pltpu.VMEM((tiles, tall, 2 * LANES), f32),
                pltpu.VMEM((2, parts, HALO, length), f32),
                pltpu.VMEM((2, 2, SLICES, HALO, length), bf16),
                pltpu.VMEM((2, 2, tiles, 2 * HALO, LANES), bf16),
                pltpu.VMEM((2, 2, tiles, 2 * HALO, LANES), bf16),
                pltpu.VMEM((rows, 32, LANES), bf16),
                pltpu.VMEM((rows, 32, LANES), bf16),
                pltpu.VMEM((rows, 24, LANES), f32),
                pltpu.VMEM((rows, 24, LANES), f32),
                pltpu.VMEM((rows, 16, LANES), f32),
                pltpu.VMEM((rows, 16, LANES), f32),
                pltpu.SemaphoreType.DMA((5,)),
                pltpu.SemaphoreType.DMA((2, 3, 2)),
                pltpu.SemaphoreType.DMA((2, 2, 2)),
                pltpu.SemaphoreType.DMA((2,)),
                pltpu.SemaphoreType.DMA((2,)),
                pltpu.SemaphoreType.DMA((2,)),
            ],
            compiler_params=pltpu.CompilerParams(
                collective_id=0, has_side_effects=True, vmem_limit_bytes=40 * 1024 * 1024
            ),
        )(*[pltpu.with_memory_space_constraint(v, pltpu.HBM) for v in (in_flight, phase_index, absorption, jnp.asarray(high), jnp.asarray(low))])

    placed = (P("depth", None, "rows", None), P("depth", "rows", None), P("depth", "rows", None))
    return jax.shard_map(
        local, mesh=mesh, in_specs=placed, out_specs=P("depth", None, "rows", None), check_vma=False
    )
```

```python
import functools
import math

import jax
import jax.numpy as jnp
import ml_dtypes
import numpy as np
from jax import lax
from jax.experimental import pallas as pl
from jax.experimental.pallas import tpu as pltpu
from jax.sharding import PartitionSpec as P

TAYLOR = 4
SLICES = 2
HALO = 8
CHUNK = 16
PLANE_WIDTH = 4
LANES = 128
lateral = 0.22
contrast = 0.2
MESH = pl.DeviceIdType.MESH


def middle_matrices(length):
    coarse = length // LANES
    b = np.arange(LANES)
    k = np.arange(length)
    f = np.where(k < length // 2, k, k - length)
    gain = np.exp(-1j * np.pi * ((f * f) % (8 * length)) / (4 * length))
    dft = np.exp(-2j * np.pi * (np.outer(b, b) % LANES) / LANES)
    whole = np.zeros((coarse, 2 * LANES, 2 * LANES))
    for k1 in range(coarse):
        twiddle = np.exp(-2j * np.pi * b * k1 / length)
        m = (twiddle[:, None] * dft * gain[k1 + coarse * b][None, :]) @ (np.conj(dft) * np.conj(twiddle)[None, :])
        m = m / length
        whole[k1] = np.block([[m.real, m.imag], [-m.imag, m.real]])
    high = whole.astype(np.float32).astype(ml_dtypes.bfloat16)
    low = (whole - high.astype(np.float64)).astype(np.float32).astype(ml_dtypes.bfloat16)
    return high, low


def radix8(re, im, sign):
    half = math.sqrt(0.5)

    def turn(r, i):
        return (-i, r) if sign > 0 else (i, -r)

    def four(r, i):
        a, b = (r[0] + r[2], i[0] + i[2]), (r[0] - r[2], i[0] - i[2])
        c, d = (r[1] + r[3], i[1] + i[3]), (r[1] - r[3], i[1] - i[3])
        d = turn(*d)
        return [(a[0] + c[0], a[1] + c[1]), (b[0] + d[0], b[1] + d[1]), (a[0] - c[0], a[1] - c[1]), (b[0] - d[0], b[1] - d[1])]

    even = four(re[0::2], im[0::2])
    odd = four(re[1::2], im[1::2])
    s = 1.0 if sign > 0 else -1.0
    o1, o3 = odd[1], odd[3]
    odd[1] = ((o1[0] - s * o1[1]) * half, (o1[1] + s * o1[0]) * half)
    odd[2] = turn(*odd[2])
    odd[3] = ((-o3[0] - s * o3[1]) * half, (-o3[1] + s * o3[0]) * half)
    out = [(e[0] + o[0], e[1] + o[1]) for e, o in zip(even, odd)]
    out += [(e[0] - o[0], e[1] - o[1]) for e, o in zip(even, odd)]
    return [v[0] for v in out], [v[1] for v in out]


def far_first(height, width):
    def centred(v, n):
        return v if v <= n // 2 else v - n

    left = [(centred(y, height), centred(x, width)) for y in range(height) for x in range(width) if y or x]
    left.sort(key=lambda t: -(abs(t[0]) + abs(t[1])))
    order = []
    while left:
        t = left.pop(0)
        order.append(t)
        opposite = [u for u in left if (u[0] + t[0]) % height == 0 and (u[1] + t[1]) % width == 0]
        if opposite:
            left.remove(opposite[0])
            order.append(opposite[0])
    return order


def swap_quarters(vs, lane):
    low64 = lane < 64
    low32 = lax.rem(lane, 64) < 32

    def roll(x, by):
        return pltpu.roll(x, by, 1)

    a0 = jnp.where(low64, vs[0], roll(vs[2], 64))
    a2 = jnp.where(low64, roll(vs[0], 64), vs[2])
    a1 = jnp.where(low64, vs[1], roll(vs[3], 64))
    a3 = jnp.where(low64, roll(vs[1], 64), vs[3])
    return [
        jnp.where(low32, a0, roll(a1, 32)),
        jnp.where(low32, roll(a0, 96), a1),
        jnp.where(low32, a2, roll(a3, 32)),
        jnp.where(low32, roll(a2, 96), a3),
    ]


def kernel(
    groups, rows, width, field_hbm, index_hbm, loss_hbm, high_hbm, low_hbm, out_ref,
    field_ref, index_ref, loss_ref, high_ref, low_ref, term, total, coef, damp, lhs, mid,
    first_field_halo, first_spec_halo, spec_send, spec_halo,
    b_send, b_recv, c_send, c_recv, d_send, d_recv,
    load_sem, first_sems, halo_sems, b_sems, c_sems, d_sems,
):
    depth = lax.axis_index("depth")
    me = lax.axis_index("rows")
    ahead = lax.rem(depth + 1, groups)
    behind = lax.rem(depth + groups - 1, groups)
    right, left = lax.rem(me + 1, rows), lax.rem(me + rows - 1, rows)
    tiles = high_ref.shape[0]
    slab = field_ref.shape[2]
    tall = slab + 2 * HALO

    barrier = pltpu.get_barrier_semaphore()

    def greet(step, carry):
        pl.semaphore_signal(barrier, inc=1, device_id=(depth, lax.rem(me + step, rows)), device_id_type=MESH)
        return carry

    def greet_behind(step, carry):
        pl.semaphore_signal(barrier, inc=1, device_id=(behind, lax.rem(me + step, rows)), device_id_type=MESH)
        return carry

    lax.fori_loop(1, rows, greet, 0)
    pairs = ((field_hbm, field_ref), (index_hbm, index_ref), (loss_hbm, loss_ref), (high_hbm, high_ref), (low_hbm, low_ref))
    loads = [pltpu.make_async_copy(src, dst, load_sem.at[i]) for i, (src, dst) in enumerate(pairs)]
    for load in loads:
        load.start()
    lax.fori_loop(0, rows, greet_behind, 0)

    lane32 = lax.broadcasted_iota(jnp.int32, (32, LANES), 1)
    lane8 = lax.broadcasted_iota(jnp.int32, (8, LANES), 1)
    lane16 = lax.broadcasted_iota(jnp.int32, (16, LANES), 1)
    row_tall = lax.broadcasted_iota(jnp.int32, (tall, LANES), 0)
    outside = ((row_tall < HALO) & (me == 0)) | ((row_tall >= HALO + slab) & (me == rows - 1))
    lat = jnp.where(outside, 0.0, lateral)

    for slot in range(2):
        for part in range(2):
            for a in range(tiles):
                term[slot, part, a, 0:HALO] = jnp.zeros((HALO, LANES), jnp.float32)
                term[slot, part, a, tall + HALO : tall + 2 * HALO] = jnp.zeros((HALO, LANES), jnp.float32)

    own_y, own_x = me // width, lax.rem(me, width)
    height = rows // width
    order = far_first(height, width)

    def start_all(src, dst, sems, to_depth, with_self):
        for dy, dx in order + ([(0, 0)] if with_self else []):
            target = lax.rem(own_y + (dy + height), height) * width + lax.rem(own_x + (dx + width), width)
            pltpu.make_async_remote_copy(
                src_ref=src.at[target], dst_ref=dst.at[me], send_sem=sems.at[0], recv_sem=sems.at[1],
                device_id=(to_depth, target), device_id_type=MESH,
            ).start()

    def whole(src, dst, sems, with_self):
        count = rows if with_self else rows - 1
        return pltpu.make_async_remote_copy(
            src_ref=src.at[pl.ds(0, count)], dst_ref=dst.at[pl.ds(0, count)], send_sem=sems.at[0], recv_sem=sems.at[1],
            device_id=(depth, right), device_id_type=MESH,
        )

    def first_halo_copies():
        copies = []
        for side, target in ((0, left), (1, right)):
            there = 1 - side
            here = pl.ds(0 if side == 0 else slab - HALO, HALO)
            triples = (
                (field_hbm.at[0, :, here, :], first_field_halo.at[there]),
                (index_hbm.at[:, here, :], first_spec_halo.at[there, 0]),
                (loss_hbm.at[:, here, :], first_spec_halo.at[there, 1]),
            )
            for n, (src, dst) in enumerate(triples):
                copies.append(
                    pltpu.make_async_remote_copy(
                        src_ref=src, dst_ref=dst,
                        send_sem=first_sems.at[0, n, side], recv_sem=first_sems.at[1, n, there],
                        device_id=(depth, target), device_id_type=MESH,
                    )
                )
        return copies

    def halo_copies(src, dst, kind):
        copies = []
        for side, target in ((0, left), (1, right)):
            there = 1 - side
            copies.append(
                pltpu.make_async_remote_copy(
                    src_ref=src.at[side], dst_ref=dst.at[there],
                    send_sem=halo_sems.at[0, kind, side], recv_sem=halo_sems.at[1, kind, there],
                    device_id=(depth, target), device_id_type=MESH,
                )
            )
        return copies

    def put_coefficients(tick, a, values):
        for k in range(SLICES):
            coef[tick, k, a, HALO : HALO + slab] = (contrast / lateral) * values[k] - 4.0
            damp[tick, k, a, HALO : HALO + slab] = (contrast / lateral) * values[SLICES + k]

    def put_spec_edges(a, values):
        for kind in range(2):
            first, second = values[SLICES * kind], values[SLICES * kind + 1]
            top = jnp.concatenate([first[:HALO], second[:HALO]], axis=0)
            bottom = jnp.concatenate([first[slab - HALO :], second[slab - HALO :]], axis=0)
            spec_send[0, kind, a] = top.astype(jnp.bfloat16)
            spec_send[1, kind, a] = bottom.astype(jnp.bfloat16)

    def use_halos(tick, field_of, spec_of):
        for side, start in ((0, 0), (1, HALO + slab)):
            off = (me == 0) if side == 0 else (me == rows - 1)
            keep = jnp.where(off, 0.0, 1.0)
            for a in range(tiles):
                for part in range(2) if field_of else ():
                    term[0, part, a, HALO + start : 2 * HALO + start] = field_of(side, part, a) * keep
                for k in range(SLICES):
                    coef[tick, k, a, start : start + HALO] = (contrast / lateral) * spec_of(side, 0, k, a) - 4.0
                    damp[tick, k, a, start : start + HALO] = (contrast / lateral) * spec_of(side, 1, k, a)

    lane_chunk = lax.broadcasted_iota(jnp.int32, (CHUNK, LANES), 1)
    first_lane = lane_chunk == 0
    last_lane = lane_chunk == LANES - 1
    nothing = jnp.zeros((CHUNK, LANES), jnp.float32)

    def one_term(tick, k, degree):
        src, dst = (degree - 1) % 2, degree % 2
        scale = 1.0 / degree
        final = k == SLICES - 1 and degree == TAYLOR
        for r in range(HALO if final else 0, HALO + slab if final else tall, CHUNK):
            at = slice(r, r + CHUNK)
            lo, hi = HALO + r, HALO + r + CHUNK
            plus, minus = lat[at] * scale, lat[at] * (-scale)

            def fetch(a):
                if a < 0 or a >= tiles:
                    return [(nothing, nothing, nothing)] * 2
                xs = [term[src, part, a, lo:hi] for part in range(2)]
                return [(x, pltpu.roll(x, 1, 1), pltpu.roll(x, LANES - 1, 1)) for x in xs]

            before, here = fetch(-1), fetch(0)
            for a in range(tiles):
                after = fetch(a + 1)
                stirred = []
                for part in range(2):
                    west = jnp.where(first_lane, before[part][1], here[part][1])
                    east = jnp.where(last_lane, after[part][2], here[part][2])
                    beside = term[src, part, a, lo - 1 : hi - 1] + term[src, part, a, lo + 1 : hi + 1]
                    stirred.append((beside + (west + east)) + coef[tick, k, a, at] * here[part][0])
                loss = damp[tick, k, a, at]
                new = [
                    (stirred[1] + loss * here[0][0]) * minus,
                    (stirred[0] - loss * here[1][0]) * plus,
                ]
                for part in range(2):
                    so_far = here[part][0] if degree == 1 else total[part, a, at]
                    if degree < TAYLOR:
                        term[dst, part, a, lo:hi] = new[part]
                        total[part, a, at] = so_far + new[part]
                    else:
                        term[dst, part, a, lo:hi] = so_far + new[part]
                before, here = here, after

    def march(tick):
        for k in range(SLICES):
            for degree in range(1, TAYLOR + 1):
                one_term(tick, k, degree)

    def convolve(load, store, slab=slab):
        for chunk in range(0, slab, 16):
            re = [load(0, a, chunk, 16) for a in range(tiles)]
            im = [load(1, a, chunk, 16) for a in range(tiles)]
            re, im = radix8(re, im, -1)
            for k1 in range(tiles):
                for part, value in ((0, re[k1]), (1, im[k1])):
                    at = slice(part * LANES, (part + 1) * LANES)
                    top = value.astype(jnp.bfloat16)
                    lhs[k1, chunk : chunk + 16, at] = top
                    lhs[k1, slab + chunk : slab + chunk + 16, at] = (value - top.astype(jnp.float32)).astype(jnp.bfloat16)
        for k1 in range(tiles):
            both = jnp.dot(lhs[k1, : 2 * slab], high_ref[k1], preferred_element_type=jnp.float32)
            rest = jnp.dot(lhs[k1, :slab], low_ref[k1], preferred_element_type=jnp.float32)
            mid[k1, :slab] = both[:slab] + (both[slab:] + rest)
        for chunk in range(0, slab, 16):
            re = [mid[k1, chunk : chunk + 16, :LANES] for k1 in range(tiles)]
            im = [mid[k1, chunk : chunk + 16, LANES:] for k1 in range(tiles)]
            re, im = radix8(re, im, 1)
            for a in range(tiles):
                store(0, a, chunk, 16, re[a])
                store(1, a, chunk, 16, im[a])

    def load_term(part, a, start, size):
        return term[0, part, a, 2 * HALO + start : 2 * HALO + start + size]

    def store_total(part, a, start, size, value):
        total[part, a, start : start + size] = value

    def load_total(part, a, start, size):
        return total[part, a, start : start + size]

    def pack(send):
        low64 = lane16 < 64
        for a in range(0, tiles, 2):
            stack = jnp.concatenate(
                [total[0, a, :slab], total[1, a, :slab], total[0, a + 1, :slab], total[1, a + 1, :slab]], axis=0
            )
            turned = stack.T
            for j in range(4):
                upper = turned[32 * j : 32 * j + 16]
                lower = turned[32 * j + 16 : 32 * j + 32]
                send[4 * a + j, 0:16] = jnp.where(low64, upper, pltpu.roll(lower, 64, 1))
                send[4 * (a + 1) + j, 0:16] = jnp.where(low64, pltpu.roll(upper, 64, 1), lower)

    def unpack(recv, first):
        for t in range(tiles):
            outs = swap_quarters([recv[4 * t + u, 0:16] for u in range(4)], lane16)
            for c_high in range(2):
                for part in range(2):
                    at = first + 16 * c_high
                    total[part, t, at : at + 16] = outs[2 * c_high + part]

    def pack_halos(send):
        low = lane8 < 64
        for r in range(rows):
            joined = jnp.where(low, send[(r + 1) % rows, 0:8], send[(r + rows - 1) % rows, 8:16])
            send[r, 16:24] = pltpu.roll(joined, 64, 1)

    def unpack_halos(recv):
        keeps = [jnp.where(me == edge_at, 0.0, 1.0) for edge_at in (0, rows - 1)]
        for t in range(tiles):
            outs = swap_quarters([recv[4 * t + u, 16:24] for u in range(4)], lane8)
            for side, start in ((0, 0), (1, HALO + slab)):
                for part in range(2):
                    total[part, t, start : start + HALO] = outs[2 * side + part] * keeps[side]

    def specimen(a):
        at = slice(a * LANES, (a + 1) * LANES)
        return [ref[k, :, at].astype(jnp.float32) for ref in (index_ref, loss_ref) for k in range(SLICES)]

    def pack_specimen():
        for a in range(tiles):
            turned = jnp.concatenate(specimen(a), axis=0).T
            for j in range(4):
                b_send[4 * a + j] = turned[32 * j : 32 * j + 32].astype(jnp.bfloat16)
        b_recv[me] = b_send[me]

    def enter():
        pl.semaphore_wait(barrier, 2 * rows - 1)
        for copy in first_halo_copies():
            copy.start()

    for load in loads[1:3]:
        load.wait()
    pack_specimen()
    enter()
    start_all(b_send, b_recv, b_sems, depth, False)
    loads[0].wait()
    for a in range(tiles):
        for part in range(2):
            term[0, part, a, 2 * HALO : 2 * HALO + slab] = field_ref[0, part, :, a * LANES : (a + 1) * LANES]
        put_coefficients(0, a, specimen(a))

    for copy in first_halo_copies():
        copy.wait_recv()
    use_halos(
        0,
        lambda side, part, a: first_field_halo[side, part, :, a * LANES : (a + 1) * LANES],
        lambda side, kind, k, a: first_spec_halo[side, kind, k, :, a * LANES : (a + 1) * LANES].astype(jnp.float32),
    )
    march(0)
    for load in loads[3:]:
        load.wait()
    convolve(load_term, store_total)
    pack(c_send)
    pack_halos(c_send)
    start_all(c_send, c_recv, c_sems, ahead, True)

    whole(b_send, b_recv, b_sems, False).wait_recv()
    for t in range(tiles):
        outs = swap_quarters([b_recv[4 * t + u].astype(jnp.float32) for u in range(4)], lane32)
        put_coefficients(1, t, outs)
        put_spec_edges(t, outs)
    spec_copies = halo_copies(spec_send, spec_halo, 1)
    for copy in spec_copies:
        copy.start()

    whole(c_send, c_recv, c_sems, True).wait_recv()
    unpack(c_recv, HALO)
    unpack_halos(c_recv)

    def store_field(part, a, start, size, value):
        term[0, part, a, HALO + start : HALO + start + size] = value

    convolve(load_total, store_field, tall)
    for copy in spec_copies:
        copy.wait_recv()
    use_halos(
        1,
        None,
        lambda side, kind, k, a: spec_halo[side, kind, a].astype(jnp.float32)[k * HALO : (k + 1) * HALO],
    )
    march(1)
    convolve(load_term, store_total)
    pack(d_send)
    start_all(d_send, d_recv, d_sems, depth, False)
    d_recv[me] = d_send[me]
    whole(d_send, d_recv, d_sems, False).wait_recv()
    unpack(d_recv, 0)

    def store_out(part, a, start, size, value):
        out_ref[0, part, start : start + size, a * LANES : (a + 1) * LANES] = value

    convolve(load_total, store_out)

    for copy in first_halo_copies() + spec_copies:
        copy.wait_send()
    whole(b_send, b_recv, b_sems, False).wait_send()
    whole(c_send, c_recv, c_sems, True).wait_send()
    whole(d_send, d_recv, d_sems, False).wait_send()


def solution(mesh):
    groups, rows = mesh.shape["depth"], mesh.shape["rows"]

    def local(in_flight, phase_index, absorption):
        _, parts, slab, length = in_flight.shape
        tiles = length // LANES
        tall = slab + 2 * HALO
        high, low = middle_matrices(length)
        f32, bf16 = jnp.float32, jnp.bfloat16
        vmem = pl.BlockSpec(memory_space=pltpu.VMEM)
        return pl.pallas_call(
            functools.partial(kernel, groups, rows, PLANE_WIDTH),
            out_shape=jax.ShapeDtypeStruct(in_flight.shape, f32),
            in_specs=[pl.BlockSpec(memory_space=pltpu.HBM)] * 5,
            out_specs=vmem,
            scratch_shapes=[
                pltpu.VMEM(in_flight.shape, f32),
                pltpu.VMEM(phase_index.shape, bf16),
                pltpu.VMEM(absorption.shape, bf16),
                pltpu.VMEM(high.shape, bf16),
                pltpu.VMEM(low.shape, bf16),
                pltpu.VMEM((2, parts, tiles, tall + 2 * HALO, LANES), f32),
                pltpu.VMEM((parts, tiles, tall, LANES), f32),
                pltpu.VMEM((2, SLICES, tiles, tall, LANES), f32),
                pltpu.VMEM((2, SLICES, tiles, tall, LANES), f32),
                pltpu.VMEM((tiles, 2 * tall, 2 * LANES), bf16),
                pltpu.VMEM((tiles, tall, 2 * LANES), f32),
                pltpu.VMEM((2, parts, HALO, length), f32),
                pltpu.VMEM((2, 2, SLICES, HALO, length), bf16),
                pltpu.VMEM((2, 2, tiles, 2 * HALO, LANES), bf16),
                pltpu.VMEM((2, 2, tiles, 2 * HALO, LANES), bf16),
                pltpu.VMEM((rows, 32, LANES), bf16),
                pltpu.VMEM((rows, 32, LANES), bf16),
                pltpu.VMEM((rows, 24, LANES), f32),
                pltpu.VMEM((rows, 24, LANES), f32),
                pltpu.VMEM((rows, 16, LANES), f32),
                pltpu.VMEM((rows, 16, LANES), f32),
                pltpu.SemaphoreType.DMA((5,)),
                pltpu.SemaphoreType.DMA((2, 3, 2)),
                pltpu.SemaphoreType.DMA((2, 2, 2)),
                pltpu.SemaphoreType.DMA((2,)),
                pltpu.SemaphoreType.DMA((2,)),
                pltpu.SemaphoreType.DMA((2,)),
            ],
            compiler_params=pltpu.CompilerParams(
                collective_id=0, has_side_effects=True, vmem_limit_bytes=40 * 1024 * 1024
            ),
        )(*[pltpu.with_memory_space_constraint(v, pltpu.HBM) for v in (in_flight, phase_index, absorption, jnp.asarray(high), jnp.asarray(low))])

    placed = (P("depth", None, "rows", None), P("depth", "rows", None), P("depth", "rows", None))
    return jax.shard_map(
        local, mesh=mesh, in_specs=placed, out_specs=P("depth", None, "rows", None), check_vma=False
    )
```

```python
import functools
import math

import jax
import jax.numpy as jnp
import ml_dtypes
import numpy as np
from jax import lax
from jax.experimental import pallas as pl
from jax.experimental.pallas import tpu as pltpu
from jax.sharding import PartitionSpec as P

TAYLOR = 4
SLICES = 2
HALO = 8
CHUNK = 16
PLANE_WIDTH = 4
LANES = 128
lateral = 0.22
contrast = 0.2
MESH = pl.DeviceIdType.MESH


def middle_matrices(length):
    coarse = length // LANES
    b = np.arange(LANES)
    k = np.arange(length)
    f = np.where(k < length // 2, k, k - length)
    gain = np.exp(-1j * np.pi * ((f * f) % (8 * length)) / (4 * length))
    dft = np.exp(-2j * np.pi * (np.outer(b, b) % LANES) / LANES)
    whole = np.zeros((coarse, 2 * LANES, 2 * LANES))
    for k1 in range(coarse):
        twiddle = np.exp(-2j * np.pi * b * k1 / length)
        m = (twiddle[:, None] * dft * gain[k1 + coarse * b][None, :]) @ (np.conj(dft) * np.conj(twiddle)[None, :])
        m = m / length
        whole[k1] = np.block([[m.real, m.imag], [-m.imag, m.real]])
    high = whole.astype(np.float32).astype(ml_dtypes.bfloat16)
    low = (whole - high.astype(np.float64)).astype(np.float32).astype(ml_dtypes.bfloat16)
    return high, low


def radix8(re, im, sign):
    half = math.sqrt(0.5)

    def turn(r, i):
        return (-i, r) if sign > 0 else (i, -r)

    def four(r, i):
        a, b = (r[0] + r[2], i[0] + i[2]), (r[0] - r[2], i[0] - i[2])
        c, d = (r[1] + r[3], i[1] + i[3]), (r[1] - r[3], i[1] - i[3])
        d = turn(*d)
        return [(a[0] + c[0], a[1] + c[1]), (b[0] + d[0], b[1] + d[1]), (a[0] - c[0], a[1] - c[1]), (b[0] - d[0], b[1] - d[1])]

    even = four(re[0::2], im[0::2])
    odd = four(re[1::2], im[1::2])
    s = 1.0 if sign > 0 else -1.0
    o1, o3 = odd[1], odd[3]
    odd[1] = ((o1[0] - s * o1[1]) * half, (o1[1] + s * o1[0]) * half)
    odd[2] = turn(*odd[2])
    odd[3] = ((-o3[0] - s * o3[1]) * half, (-o3[1] + s * o3[0]) * half)
    out = [(e[0] + o[0], e[1] + o[1]) for e, o in zip(even, odd)]
    out += [(e[0] - o[0], e[1] - o[1]) for e, o in zip(even, odd)]
    return [v[0] for v in out], [v[1] for v in out]


def far_first(height, width):
    def centred(v, n):
        return v if v <= n // 2 else v - n

    left = [(centred(y, height), centred(x, width)) for y in range(height) for x in range(width) if y or x]
    left.sort(key=lambda t: -(abs(t[0]) + abs(t[1])))
    order = []
    while left:
        t = left.pop(0)
        order.append(t)
        opposite = [u for u in left if (u[0] + t[0]) % height == 0 and (u[1] + t[1]) % width == 0]
        if opposite:
            left.remove(opposite[0])
            order.append(opposite[0])
    return order


def swap_quarters(vs, lane):
    low64 = lane < 64
    low32 = lax.rem(lane, 64) < 32

    def roll(x, by):
        return pltpu.roll(x, by, 1)

    a0 = jnp.where(low64, vs[0], roll(vs[2], 64))
    a2 = jnp.where(low64, roll(vs[0], 64), vs[2])
    a1 = jnp.where(low64, vs[1], roll(vs[3], 64))
    a3 = jnp.where(low64, roll(vs[1], 64), vs[3])
    return [
        jnp.where(low32, a0, roll(a1, 32)),
        jnp.where(low32, roll(a0, 96), a1),
        jnp.where(low32, a2, roll(a3, 32)),
        jnp.where(low32, roll(a2, 96), a3),
    ]


def kernel(
    groups, rows, width, field_hbm, index_hbm, loss_hbm, high_hbm, low_hbm, out_ref,
    field_ref, index_ref, loss_ref, high_ref, low_ref, term, total, coef, damp, lhs, mid,
    first_field_halo, first_spec_halo, spec_send, spec_halo,
    b_send, b_recv, c_send, c_recv, d_send, d_recv,
    load_sem, first_sems, halo_sems, b_sems, c_sems, d_sems,
):
    depth = lax.axis_index("depth")
    me = lax.axis_index("rows")
    ahead = lax.rem(depth + 1, groups)
    behind = lax.rem(depth + groups - 1, groups)
    right, left = lax.rem(me + 1, rows), lax.rem(me + rows - 1, rows)
    tiles = high_ref.shape[0]
    slab = field_ref.shape[2]
    tall = slab + 2 * HALO

    barrier = pltpu.get_barrier_semaphore()

    def greet(step, carry):
        pl.semaphore_signal(barrier, inc=1, device_id=(depth, lax.rem(me + step, rows)), device_id_type=MESH)
        return carry

    def greet_behind(step, carry):
        pl.semaphore_signal(barrier, inc=1, device_id=(behind, lax.rem(me + step, rows)), device_id_type=MESH)
        return carry

    lax.fori_loop(1, rows, greet, 0)
    pairs = ((field_hbm, field_ref), (index_hbm, index_ref), (loss_hbm, loss_ref), (high_hbm, high_ref), (low_hbm, low_ref))
    loads = [pltpu.make_async_copy(src, dst, load_sem.at[i]) for i, (src, dst) in enumerate(pairs)]
    for load in loads:
        load.start()
    lax.fori_loop(0, rows, greet_behind, 0)

    lane32 = lax.broadcasted_iota(jnp.int32, (32, LANES), 1)
    lane8 = lax.broadcasted_iota(jnp.int32, (8, LANES), 1)
    lane16 = lax.broadcasted_iota(jnp.int32, (16, LANES), 1)
    row_tall = lax.broadcasted_iota(jnp.int32, (tall, LANES), 0)
    outside = ((row_tall < HALO) & (me == 0)) | ((row_tall >= HALO + slab) & (me == rows - 1))
    lat = jnp.where(outside, 0.0, lateral)
    lat_slab = jnp.full((slab, LANES), lateral, jnp.float32)

    for slot in range(2):
        for part in range(2):
            for a in range(tiles):
                term[slot, part, a, 0:HALO] = jnp.zeros((HALO, LANES), jnp.float32)
                term[slot, part, a, tall + HALO : tall + 2 * HALO] = jnp.zeros((HALO, LANES), jnp.float32)

    own_y, own_x = me // width, lax.rem(me, width)
    height = rows // width
    order = far_first(height, width)

    def start_all(src, dst, sems, to_depth, with_self):
        for dy, dx in order + ([(0, 0)] if with_self else []):
            target = lax.rem(own_y + (dy + height), height) * width + lax.rem(own_x + (dx + width), width)
            pltpu.make_async_remote_copy(
                src_ref=src.at[target], dst_ref=dst.at[me], send_sem=sems.at[0], recv_sem=sems.at[1],
                device_id=(to_depth, target), device_id_type=MESH,
            ).start()

    def whole(src, dst, sems, with_self):
        count = rows if with_self else rows - 1
        return pltpu.make_async_remote_copy(
            src_ref=src.at[pl.ds(0, count)], dst_ref=dst.at[pl.ds(0, count)], send_sem=sems.at[0], recv_sem=sems.at[1],
            device_id=(depth, right), device_id_type=MESH,
        )

    def first_halo_copies():
        copies = []
        for side, target in ((0, left), (1, right)):
            there = 1 - side
            here = pl.ds(0 if side == 0 else slab - HALO, HALO)
            triples = (
                (field_hbm.at[0, :, here, :], first_field_halo.at[there]),
                (index_hbm.at[:, here, :], first_spec_halo.at[there, 0]),
                (loss_hbm.at[:, here, :], first_spec_halo.at[there, 1]),
            )
            for n, (src, dst) in enumerate(triples):
                copies.append(
                    pltpu.make_async_remote_copy(
                        src_ref=src, dst_ref=dst,
                        send_sem=first_sems.at[0, n, side], recv_sem=first_sems.at[1, n, there],
                        device_id=(depth, target), device_id_type=MESH,
                    )
                )
        return copies[0::3] + copies[1::3] + copies[2::3]

    def halo_copies(src, dst, kind):
        copies = []
        for side, target in ((0, left), (1, right)):
            there = 1 - side
            copies.append(
                pltpu.make_async_remote_copy(
                    src_ref=src.at[side], dst_ref=dst.at[there],
                    send_sem=halo_sems.at[0, kind, side], recv_sem=halo_sems.at[1, kind, there],
                    device_id=(depth, target), device_id_type=MESH,
                )
            )
        return copies

    def put_coefficients(tick, a, values):
        for k in range(SLICES):
            coef[tick, k, a, HALO : HALO + slab] = contrast * values[k] - 4.0 * lat_slab
            damp[tick, k, a, HALO : HALO + slab] = contrast * values[SLICES + k]

    def put_spec_edges(a, values):
        for kind in range(2):
            first, second = values[SLICES * kind], values[SLICES * kind + 1]
            top = jnp.concatenate([first[:HALO], second[:HALO]], axis=0)
            bottom = jnp.concatenate([first[slab - HALO :], second[slab - HALO :]], axis=0)
            spec_send[0, kind, a] = top.astype(jnp.bfloat16)
            spec_send[1, kind, a] = bottom.astype(jnp.bfloat16)

    def use_halos(tick, field_of, spec_of):
        for side, start in ((0, 0), (1, HALO + slab)):
            off = (me == 0) if side == 0 else (me == rows - 1)
            keep = jnp.where(off, 0.0, 1.0)
            lat_here = lateral * keep
            for a in range(tiles):
                for part in range(2) if field_of else ():
                    term[0, part, a, HALO + start : 2 * HALO + start] = field_of(side, part, a) * keep
                for k in range(SLICES):
                    coef[tick, k, a, start : start + HALO] = contrast * spec_of(side, 0, k, a) - 4.0 * lat_here
                    damp[tick, k, a, start : start + HALO] = contrast * spec_of(side, 1, k, a)

    lane_chunk = lax.broadcasted_iota(jnp.int32, (CHUNK, LANES), 1)
    first_lane = lane_chunk == 0
    last_lane = lane_chunk == LANES - 1
    nothing = jnp.zeros((CHUNK, LANES), jnp.float32)

    def one_term(tick, k, degree):
        src, dst = (degree - 1) % 2, degree % 2
        scale = 1.0 / degree
        final = k == SLICES - 1 and degree == TAYLOR
        for r in range(HALO if final else 0, HALO + slab if final else tall, CHUNK):
            at = slice(r, r + CHUNK)
            lo, hi = HALO + r, HALO + r + CHUNK

            def fetch(a):
                if a < 0 or a >= tiles:
                    return [(nothing, nothing, nothing)] * 2
                xs = [term[src, part, a, lo:hi] for part in range(2)]
                return [(x, pltpu.roll(x, 1, 1), pltpu.roll(x, LANES - 1, 1)) for x in xs]

            before, here = fetch(-1), fetch(0)
            for a in range(tiles):
                after = fetch(a + 1)
                stirred = []
                for part in range(2):
                    west = jnp.where(first_lane, before[part][1], here[part][1])
                    east = jnp.where(last_lane, after[part][2], here[part][2])
                    beside = term[src, part, a, lo - 1 : hi - 1] + term[src, part, a, lo + 1 : hi + 1]
                    stirred.append(lat[at] * (beside + (west + east)) + coef[tick, k, a, at] * here[part][0])
                loss = damp[tick, k, a, at]
                new = [
                    (stirred[1] + loss * here[0][0]) * (-scale),
                    (stirred[0] - loss * here[1][0]) * scale,
                ]
                for part in range(2):
                    so_far = here[part][0] if degree == 1 else total[part, a, at]
                    if degree < TAYLOR:
                        term[dst, part, a, lo:hi] = new[part]
                        total[part, a, at] = so_far + new[part]
                    else:
                        term[dst, part, a, lo:hi] = so_far + new[part]
                before, here = here, after

    def march(tick):
        for k in range(SLICES):
            for degree in range(1, TAYLOR + 1):
                one_term(tick, k, degree)

    def convolve(load, store, slab=slab):
        for chunk in range(0, slab, 16):
            re = [load(0, a, chunk, 16) for a in range(tiles)]
            im = [load(1, a, chunk, 16) for a in range(tiles)]
            re, im = radix8(re, im, -1)
            for k1 in range(tiles):
                for part, value in ((0, re[k1]), (1, im[k1])):
                    at = slice(part * LANES, (part + 1) * LANES)
                    top = value.astype(jnp.bfloat16)
                    lhs[k1, chunk : chunk + 16, at] = top
                    lhs[k1, slab + chunk : slab + chunk + 16, at] = (value - top.astype(jnp.float32)).astype(jnp.bfloat16)
        for k1 in range(tiles):
            both = jnp.dot(lhs[k1, : 2 * slab], high_ref[k1], preferred_element_type=jnp.float32)
            rest = jnp.dot(lhs[k1, :slab], low_ref[k1], preferred_element_type=jnp.float32)
            mid[k1, :slab] = both[:slab] + (both[slab:] + rest)
        for chunk in range(0, slab, 16):
            re = [mid[k1, chunk : chunk + 16, :LANES] for k1 in range(tiles)]
            im = [mid[k1, chunk : chunk + 16, LANES:] for k1 in range(tiles)]
            re, im = radix8(re, im, 1)
            for a in range(tiles):
                store(0, a, chunk, 16, re[a])
                store(1, a, chunk, 16, im[a])

    def load_term(part, a, start, size):
        return term[0, part, a, 2 * HALO + start : 2 * HALO + start + size]

    def store_total(part, a, start, size, value):
        total[part, a, start : start + size] = value

    def load_total(part, a, start, size):
        return total[part, a, start : start + size]

    def pack(send):
        low64 = lane16 < 64
        for a in range(0, tiles, 2):
            stack = jnp.concatenate(
                [total[0, a, :slab], total[1, a, :slab], total[0, a + 1, :slab], total[1, a + 1, :slab]], axis=0
            )
            turned = stack.T
            for j in range(4):
                upper = turned[32 * j : 32 * j + 16]
                lower = turned[32 * j + 16 : 32 * j + 32]
                send[4 * a + j, 0:16] = jnp.where(low64, upper, pltpu.roll(lower, 64, 1))
                send[4 * (a + 1) + j, 0:16] = jnp.where(low64, pltpu.roll(upper, 64, 1), lower)

    def unpack(recv, first):
        for t in range(tiles):
            outs = swap_quarters([recv[4 * t + u, 0:16] for u in range(4)], lane16)
            for c_high in range(2):
                for part in range(2):
                    at = first + 16 * c_high
                    total[part, t, at : at + 16] = outs[2 * c_high + part]

    def pack_halos(send):
        low = lane8 < 64
        for r in range(rows):
            joined = jnp.where(low, send[(r + 1) % rows, 0:8], send[(r + rows - 1) % rows, 8:16])
            send[r, 16:24] = pltpu.roll(joined, 64, 1)

    def unpack_halos(recv):
        keeps = [jnp.where(me == edge_at, 0.0, 1.0) for edge_at in (0, rows - 1)]
        for t in range(tiles):
            outs = swap_quarters([recv[4 * t + u, 16:24] for u in range(4)], lane8)
            for side, start in ((0, 0), (1, HALO + slab)):
                for part in range(2):
                    total[part, t, start : start + HALO] = outs[2 * side + part] * keeps[side]

    def specimen(a):
        at = slice(a * LANES, (a + 1) * LANES)
        return [ref[k, :, at].astype(jnp.float32) for ref in (index_ref, loss_ref) for k in range(SLICES)]

    def pack_specimen():
        for a in range(tiles):
            turned = jnp.concatenate(specimen(a), axis=0).T
            for j in range(4):
                b_send[4 * a + j] = turned[32 * j : 32 * j + 32].astype(jnp.bfloat16)
        b_recv[me] = b_send[me]

    def enter():
        pl.semaphore_wait(barrier, 2 * rows - 1)
        for copy in first_halo_copies():
            copy.start()

    for load in loads[1:3]:
        load.wait()
    pack_specimen()
    enter()
    start_all(b_send, b_recv, b_sems, depth, False)
    loads[0].wait()
    for a in range(tiles):
        for part in range(2):
            term[0, part, a, 2 * HALO : 2 * HALO + slab] = field_ref[0, part, :, a * LANES : (a + 1) * LANES]
        put_coefficients(0, a, specimen(a))

    for copy in first_halo_copies():
        copy.wait_recv()
    use_halos(
        0,
        lambda side, part, a: first_field_halo[side, part, :, a * LANES : (a + 1) * LANES],
        lambda side, kind, k, a: first_spec_halo[side, kind, k, :, a * LANES : (a + 1) * LANES].astype(jnp.float32),
    )
    march(0)
    for load in loads[3:]:
        load.wait()
    convolve(load_term, store_total)
    pack(c_send)
    pack_halos(c_send)
    start_all(c_send, c_recv, c_sems, ahead, True)

    whole(b_send, b_recv, b_sems, False).wait_recv()
    for t in range(tiles):
        outs = swap_quarters([b_recv[4 * t + u].astype(jnp.float32) for u in range(4)], lane32)
        put_coefficients(1, t, outs)
        put_spec_edges(t, outs)
    spec_copies = halo_copies(spec_send, spec_halo, 1)
    for copy in spec_copies:
        copy.start()

    whole(c_send, c_recv, c_sems, True).wait_recv()
    unpack(c_recv, HALO)
    unpack_halos(c_recv)

    def store_field(part, a, start, size, value):
        term[0, part, a, HALO + start : HALO + start + size] = value

    convolve(load_total, store_field, tall)
    for copy in spec_copies:
        copy.wait_recv()
    use_halos(
        1,
        None,
        lambda side, kind, k, a: spec_halo[side, kind, a].astype(jnp.float32)[k * HALO : (k + 1) * HALO],
    )
    march(1)
    convolve(load_term, store_total)
    pack(d_send)
    start_all(d_send, d_recv, d_sems, depth, False)
    d_recv[me] = d_send[me]
    whole(d_send, d_recv, d_sems, False).wait_recv()
    unpack(d_recv, 0)

    def store_out(part, a, start, size, value):
        out_ref[0, part, start : start + size, a * LANES : (a + 1) * LANES] = value

    convolve(load_total, store_out)

    for copy in first_halo_copies() + spec_copies:
        copy.wait_send()
    whole(b_send, b_recv, b_sems, False).wait_send()
    whole(c_send, c_recv, c_sems, True).wait_send()
    whole(d_send, d_recv, d_sems, False).wait_send()


def solution(mesh):
    groups, rows = mesh.shape["depth"], mesh.shape["rows"]

    def local(in_flight, phase_index, absorption):
        _, parts, slab, length = in_flight.shape
        tiles = length // LANES
        tall = slab + 2 * HALO
        high, low = middle_matrices(length)
        f32, bf16 = jnp.float32, jnp.bfloat16
        vmem = pl.BlockSpec(memory_space=pltpu.VMEM)
        return pl.pallas_call(
            functools.partial(kernel, groups, rows, PLANE_WIDTH),
            out_shape=jax.ShapeDtypeStruct(in_flight.shape, f32),
            in_specs=[pl.BlockSpec(memory_space=pltpu.HBM)] * 5,
            out_specs=vmem,
            scratch_shapes=[
                pltpu.VMEM(in_flight.shape, f32),
                pltpu.VMEM(phase_index.shape, bf16),
                pltpu.VMEM(absorption.shape, bf16),
                pltpu.VMEM(high.shape, bf16),
                pltpu.VMEM(low.shape, bf16),
                pltpu.VMEM((2, parts, tiles, tall + 2 * HALO, LANES), f32),
                pltpu.VMEM((parts, tiles, tall, LANES), f32),
                pltpu.VMEM((2, SLICES, tiles, tall, LANES), f32),
                pltpu.VMEM((2, SLICES, tiles, tall, LANES), f32),
                pltpu.VMEM((tiles, 2 * tall, 2 * LANES), bf16),
                pltpu.VMEM((tiles, tall, 2 * LANES), f32),
                pltpu.VMEM((2, parts, HALO, length), f32),
                pltpu.VMEM((2, 2, SLICES, HALO, length), bf16),
                pltpu.VMEM((2, 2, tiles, 2 * HALO, LANES), bf16),
                pltpu.VMEM((2, 2, tiles, 2 * HALO, LANES), bf16),
                pltpu.VMEM((rows, 32, LANES), bf16),
                pltpu.VMEM((rows, 32, LANES), bf16),
                pltpu.VMEM((rows, 24, LANES), f32),
                pltpu.VMEM((rows, 24, LANES), f32),
                pltpu.VMEM((rows, 16, LANES), f32),
                pltpu.VMEM((rows, 16, LANES), f32),
                pltpu.SemaphoreType.DMA((5,)),
                pltpu.SemaphoreType.DMA((2, 3, 2)),
                pltpu.SemaphoreType.DMA((2, 2, 2)),
                pltpu.SemaphoreType.DMA((2,)),
                pltpu.SemaphoreType.DMA((2,)),
                pltpu.SemaphoreType.DMA((2,)),
            ],
            compiler_params=pltpu.CompilerParams(
                collective_id=0, has_side_effects=True, vmem_limit_bytes=40 * 1024 * 1024
            ),
        )(*[pltpu.with_memory_space_constraint(v, pltpu.HBM) for v in (in_flight, phase_index, absorption, jnp.asarray(high), jnp.asarray(low))])

    placed = (P("depth", None, "rows", None), P("depth", "rows", None), P("depth", "rows", None))
    return jax.shard_map(
        local, mesh=mesh, in_specs=placed, out_specs=P("depth", None, "rows", None), check_vma=False
    )
```
